512 devices in a mesh: grp: 8 (over z), slab: 64 (over y, x, core).
Axes of the slice: x: 4, y: 8, z: 8, core: 2. Of those that a mesh axis runs over, the one named last changes fastest.
Arguments:
- thermal_state_values: float32 [1024, 512], P(('grp', 'slab')), may hold values from -6 to 6
- thermal_kappa_values: float32 [512, 128], P(('grp', 'slab')), may hold values from 0.5 to 2
- nodal_heating_input: float32 [1024, 512], P(('grp', 'slab')), may hold values from -24 to 24
- frozen_share_map: float32 [4096, 8192], P('grp', 'slab'), may hold values from 0 to 1
- crystal_label_map: int32 [4096, 8192], P('grp', 'slab'), may hold values from 0 to 7999
- growth_reach_table: int32 [8000, 6], replicated, may hold values from 1 to 4
- seed_site_slots: int32 [131072], P(('grp', 'slab')), may hold values from 0 to 65535
- seed_crystal_label: int32 [131072], P(('grp', 'slab')), may hold values from 0 to 7999
Outputs:
- new_temperature: float32 [1024, 512], P(('grp', 'slab'))
- new_solid: float32 [4096, 8192], P('grp', 'slab')
The draws below stay inside these ranges and needn't reach their ends.
Inputs may be any that keep to these rules, and one draw needn't show every extreme that they name: `seed_site_slots`: each entry is a cell of the brick of the device that holds the entry, numbered x * 8 * 16 + y * 16 + z in that brick's own coordinates; entries may repeat.
All inputs are finite; a program needn't handle non-finite values.
Results may differ from the reference program's by a relative error of at most 0.0001.
Values sent between devices are 32-bit elements; how exact they have to be, the bound alone decides.
A program may use at most 128 MiB of HBM per device.

```python
import math
import jax
import jax.numpy as jnp
from jax import lax

HEX_COUNT_LATER = 2
NSD = 256
CPC = 8
NORI = 8000
EY = 64
NEX = 512
POINTS_ALONG_X = 1024
POINTS_ALONG_Y = 128
POINTS_ALONG_Z = 4
NCX = 4096
NCY = 512
NCZ = 16
BX = 512
BY = 8
BCELLS = 65536
SITES = 131072
N_SLAB = 64


def plant(values, stream_key, low, high):
    longest = values.shape.index(max(values.shape))
    spots = []
    for shift in (0, 1):
        where = [jax.random.randint(jax.random.fold_in(stream_key, axis), (), 0, length) for axis, length in enumerate(values.shape)]
        where[longest] = (where[longest] + shift) % values.shape[longest]
        spots.append(tuple(where))
    return values.at[spots[0]].set(low).at[spots[1]].set(high)


def steps_of(rng, dims, split, low, top_value):
    loudness, own = 1.0, jax.random.fold_in(rng, 6)
    for position, blocks in split:
        heights = jnp.exp(jax.random.uniform(jax.random.fold_in(own, position), (blocks,), jnp.float32, low / len(split), top_value / len(split)))
        loudness = loudness * jnp.repeat(heights, dims[position] // blocks).reshape([-1 if axis == position else 1 for axis in range(len(dims))])
    return loudness


def bell_draw(rng, extent, width, bound, pieces=(), kind=jnp.bfloat16):
    values = width * jax.random.normal(rng, extent, jnp.float32)
    if pieces:
        values = values * steps_of(rng, extent, pieces, -0.22, 0.18)
    return jnp.clip(values, -bound, bound).astype(kind)


def setup_inputs(seed: int = 0) -> dict:
    arg_keys = jax.random.split(jax.random.key(seed), 9)
    return {
        "thermal_state_values": bell_draw(arg_keys[0], (POINTS_ALONG_X, POINTS_ALONG_Y * POINTS_ALONG_Z), 1.0, 6.0, ((0, 512),), jnp.float32),
        "thermal_kappa_values": jnp.clip(jnp.exp(math.log(2.0) - 1.3862944 * jax.random.uniform(arg_keys[1], (NEX, EY * HEX_COUNT_LATER), jnp.float32) ** steps_of(arg_keys[1], (NEX, EY * HEX_COUNT_LATER), ((0, 512),), -0.2, 0.2)), 0.5, 2.0),
        "nodal_heating_input": bell_draw(arg_keys[2], (POINTS_ALONG_X, POINTS_ALONG_Y * POINTS_ALONG_Z), 4.0, 24.0, ((0, 512),), jnp.float32),
        "frozen_share_map": jnp.clip(1.0 * jax.random.uniform(arg_keys[3], (NCX, NCY * NCZ), jnp.float32) ** steps_of(arg_keys[3], (NCX, NCY * NCZ), ((0, 8), (1, 64)), -0.2, 0.2), 0.0, 1.0),
        "crystal_label_map": plant(jax.random.randint(arg_keys[4], (NCX, NCY * NCZ), 0, NORI), jax.random.fold_in(arg_keys[4], 1), 0, NORI - 1).astype(jnp.int32),
        "growth_reach_table": plant(jax.random.randint(arg_keys[5], (NORI, 6), 1, 5), jax.random.fold_in(arg_keys[5], 1), 1, 4).astype(jnp.int32),
        "seed_site_slots": plant(jax.random.randint(arg_keys[6], (SITES,), 0, BCELLS), jax.random.fold_in(arg_keys[6], 1), 0, BCELLS - 1).astype(jnp.int32),
        "seed_crystal_label": plant(jax.random.randint(arg_keys[7], (SITES,), 0, NORI), jax.random.fold_in(arg_keys[7], 1), 0, NORI - 1).astype(jnp.int32),
    }


HIGHEST = lax.Precision.HIGHEST
step_size = 0.004


def stiffness_table():
    derivative = jnp.array([[-3.0, 4.0, -1.0], [-1.0, 0.0, 1.0], [1.0, -4.0, 3.0]], jnp.float32)
    quad_weight = jnp.array([1.0 / 6.0, 2.0 / 3.0, 1.0 / 6.0], jnp.float32)
    identity = jnp.eye(3, dtype=jnp.float32)
    weight_cube = jnp.kron(jnp.kron(quad_weight, quad_weight), quad_weight)
    stiffness = jnp.zeros((27, 27), jnp.float32)
    for direction in range(3):
        factors = [identity, identity, identity]
        factors[direction] = derivative
        gradient = jnp.kron(jnp.kron(factors[0], factors[1]), factors[2])
        stiffness = stiffness + jnp.dot(gradient.T * weight_cube[None, :], gradient, precision=HIGHEST)
    return stiffness


def cell_basis(length):
    points = (jnp.arange(length, dtype=jnp.float32) + 0.5) / length
    columns = jnp.stack([2.0 * (points - 0.5) * (points - 1.0), -4.0 * points * (points - 1.0), 2.0 * points * (points - 0.5)], axis=1)
    return jnp.kron(jnp.kron(columns, columns), columns)


def split_axis(tensor, which_axis, length):
    return jnp.stack([lax.slice_in_dim(tensor, offset, offset + 2 * length - 1, 2, which_axis) for offset in range(3)], 0)


def element_nodes(extended, count_x, count_y, count_z):
    tensor = split_axis(extended, 0, count_x)
    tensor = split_axis(tensor, 2, count_y)
    tensor = split_axis(tensor, 4, count_z)
    return jnp.transpose(tensor, (2, 1, 0, 3, 4, 5))


def fold_axis(tensor, which_axis, length):
    first_part, middle, last_part = tensor[0], tensor[1], tensor[2]
    place_at = which_axis - 1
    plane_shape = list(first_part.shape)
    plane_shape[place_at] = 1
    zero_plane = jnp.zeros(plane_shape, tensor.dtype)
    even_nodes = jnp.concatenate([first_part, zero_plane], place_at) + jnp.concatenate([zero_plane, last_part], place_at)
    paired = jnp.stack([lax.slice_in_dim(even_nodes, 0, length, 1, place_at), middle], place_at + 1)
    full_shape = list(first_part.shape)
    full_shape[place_at] = 2 * length
    paired = paired.reshape(full_shape)
    return jnp.concatenate([paired, lax.slice_in_dim(even_nodes, length, length + 1, 1, place_at)], place_at)


def element_action(extended, kappa, stiffness, count_x, count_y, count_z):
    nodes = element_nodes(extended, count_x, count_y, count_z).reshape(27, -1)
    acted = jnp.dot(stiffness, nodes, precision=HIGHEST) * kappa.reshape(1, -1)
    acted = acted.reshape(3, 3, 3, count_x, count_y, count_z)
    acted = jnp.transpose(acted, (2, 0, 1, 3, 4, 5))
    acted = fold_axis(acted, 5, count_z)
    acted = jnp.transpose(acted, (1, 0, 2, 3, 4))
    acted = fold_axis(acted, 3, count_y)
    return fold_axis(acted, 1, count_x)


def extend_wrap(tensor, which_axis):
    return jnp.concatenate([tensor, lax.slice_in_dim(tensor, 0, 1, 1, which_axis)], which_axis)


def fold_wrap(tensor, which_axis):
    length = tensor.shape[which_axis] - 1
    head_plane = lax.slice_in_dim(tensor, 0, 1, 1, which_axis) + lax.slice_in_dim(tensor, length, length + 1, 1, which_axis)
    return jnp.concatenate([head_plane, lax.slice_in_dim(tensor, 1, length, 1, which_axis)], which_axis)


def apply_operator(present_values, thermal_kappa_values, stiffness):
    extended = extend_wrap(extend_wrap(extend_wrap(present_values, 0), 1), 2)
    acted = element_action(extended, thermal_kappa_values, stiffness, NEX, EY, HEX_COUNT_LATER)
    return fold_wrap(fold_wrap(fold_wrap(acted, 0), 1), 2)


def node_mass(length):
    return jnp.where(jnp.arange(length) % 2 == 0, 1.0 / 3.0, 2.0 / 3.0).astype(jnp.float32)


def reference(thermal_state_values, thermal_kappa_values, nodal_heating_input, frozen_share_map, crystal_label_map, growth_reach_table, seed_site_slots, seed_crystal_label):
    stiffness = stiffness_table()
    present_values = thermal_state_values.reshape(POINTS_ALONG_X, POINTS_ALONG_Y, POINTS_ALONG_Z)
    heat_source = nodal_heating_input.reshape(POINTS_ALONG_X, POINTS_ALONG_Y, POINTS_ALONG_Z)
    lumped_mass = node_mass(POINTS_ALONG_X)[:, None, None] * node_mass(POINTS_ALONG_Y)[None, :, None] * node_mass(POINTS_ALONG_Z)[None, None, :]
    rate_one = (heat_source - apply_operator(present_values, thermal_kappa_values, stiffness)) / lumped_mass
    middle = present_values + step_size * rate_one
    rate_two = (heat_source - apply_operator(middle, thermal_kappa_values, stiffness)) / lumped_mass
    new_field = present_values + 0.5 * step_size * (rate_one + rate_two)
    extended = extend_wrap(extend_wrap(extend_wrap(new_field, 0), 1), 2)
    nodes = element_nodes(extended, NEX, EY, HEX_COUNT_LATER).reshape(27, -1)
    cell_temp = jnp.dot(cell_basis(CPC), nodes, precision=HIGHEST).reshape(CPC, CPC, CPC, NEX, EY, HEX_COUNT_LATER)
    cell_temp = jnp.transpose(cell_temp, (3, 0, 4, 1, 5, 2)).reshape(NCX, NCY, NCZ)
    undercool = jnp.maximum(-cell_temp, 0.0)
    level_table = growth_reach_table.astype(jnp.float32) / 4.0
    grid_solid = frozen_share_map.reshape(NCX, NCY, NCZ)
    grid_orient = crystal_label_map.reshape(NCX, NCY, NCZ)
    offsets = ((0, 1), (0, -1), (1, 1), (1, -1), (2, 1), (2, -1))
    gathered = jnp.zeros((NCX, NCY, NCZ), jnp.float32)
    for direction in range(6):
        which_axis, offset = offsets[direction]
        weighted = grid_solid * jnp.take(level_table[:, direction], grid_orient)
        gathered = gathered + jnp.roll(weighted, -offset, which_axis)
    mean_level = jnp.sum(growth_reach_table.astype(jnp.float32), axis=1) / 6.0
    brick_index = jnp.arange(SITES, dtype=jnp.int32) // NSD
    global_x = (brick_index // N_SLAB) * BX + seed_site_slots // (BY * NCZ)
    global_y = (brick_index % N_SLAB) * BY + (seed_site_slots // NCZ) % BY
    global_z = seed_site_slots % NCZ
    flat_index = ((global_x * NCY + global_y) * NCZ + global_z).astype(jnp.int32)
    nucleation = jnp.zeros((NCX * NCY * NCZ,), jnp.float32).at[flat_index].add(jnp.take(mean_level, seed_crystal_label))
    nucleation = nucleation.reshape(NCX, NCY, NCZ)
    capture_rate = undercool * undercool * gathered + undercool * nucleation
    new_solid = grid_solid + (1.0 - grid_solid) * (1.0 - jnp.exp(-capture_rate))
    return new_field.reshape(POINTS_ALONG_X, POINTS_ALONG_Y * POINTS_ALONG_Z), new_solid.reshape(NCX, NCY * NCZ)
```

```python
import functools

import jax
import jax.numpy as jnp
import numpy as np
from jax import lax
from jax.experimental import pallas as pl
from jax.experimental.pallas import tpu as pltpu
from jax.sharding import PartitionSpec as P

MESH = pl.DeviceIdType.MESH
HIGHEST = lax.Precision.HIGHEST
STEP = 0.004
CHUNK = 64
ROWS = 72


def interpolation_matrix():
    points = (np.arange(8) + 0.5) / 8
    basis = np.stack(
        [
            2.0 * (points - 0.5) * (points - 1.0),
            -4.0 * points * (points - 1.0),
            2.0 * points * (points - 0.5),
        ],
        1,
    )
    along_z = np.zeros((4, 16))
    for c in range(2):
        for p in range(8):
            for k in range(3):
                along_z[(2 * c + k) % 4, 8 * c + p] += basis[p, k]
    plane = np.einsum("nj,zc->jznc", basis, along_z).reshape(12, 128)
    matrix = np.zeros((128, 256), np.float32)
    matrix[16:28, :128] = plane
    matrix[80:92, 128:] = plane
    return matrix


def take_lanes(values, index):
    return jnp.take_along_axis(values, index, axis=1, mode="promise_in_bounds")


def stiffness_action(kappa, shifts):
    odd_x, odd_y, odd_z = shifts.odd

    def spread(values, axis):
        before = shifts.moved(values, axis, -1)
        return jnp.where(
            shifts.odd[axis], (2.0 / 3.0) * values, (1.0 / 6.0) * (values + before)
        )

    def spread_x(values):
        return jnp.where(
            odd_x,
            (2.0 / 3.0) * values,
            (1.0 / 6.0) * (values + shifts.slab(values, -1)),
        )

    over_x = spread_x(kappa)
    fields = (
        spread(spread(kappa, 1), 2) * (1.0 / 3.0),
        spread(over_x, 2) * (1.0 / 3.0),
        spread(over_x, 1) * (1.0 / 3.0),
    )
    centre = None
    pairs = []
    for axis in range(3):
        here = fields[axis]
        if axis == 0:
            before = shifts.slab(here, -1)
        else:
            before = shifts.moved(here, axis, -1)
        part = jnp.where(shifts.odd[axis], 16.0 * here, 7.0 * (here + before))
        centre = part if centre is None else centre + part
        pairs.append((here, jnp.where(shifts.odd[axis], here, before)))

    def act(values):
        total = centre * values
        for axis in range(3):
            ahead, behind = pairs[axis]
            one, two, back, back_two = shifts.neighbours(values, axis)
            odd = shifts.odd[axis]
            total = total + ahead * (jnp.where(odd, 0.0, two) - 8.0 * one)
            total = total + behind * (jnp.where(odd, 0.0, back_two) - 8.0 * back)
        return total

    return act


class Shifts:
    lane_axis = 1

    def lane_roll(self, values, by):
        return pltpu.roll(values, by % 128, self.lane_axis)

    def z_moved(self, values, by):
        z = self.z
        if by == 1:
            return jnp.where(z == 3, self.lane_roll(values, 3), self.lane_roll(values, -1))
        if by == -1:
            return jnp.where(z == 0, self.lane_roll(values, -3), self.lane_roll(values, 1))
        return jnp.where(z >= 2, self.lane_roll(values, 2), self.lane_roll(values, -2))

    def moved(self, values, axis, by):
        if axis == 1:
            return self.y_moved(values, by)
        return self.z_moved(values, by)

    def neighbours(self, values, axis):
        if axis == 0:
            other = self.other(values)
            ahead = jnp.where(self.odd[0], self.slab(other, 1), other)
            behind = jnp.where(self.odd[0], other, self.slab(other, -1))
            return ahead, self.slab(values, 1), behind, self.slab(values, -1)
        if axis == 1:
            return tuple(self.y_moved(values, by) for by in (1, 2, -1, -2))
        two = self.z_moved(values, 2)
        return self.z_moved(values, 1), two, self.z_moved(values, -1), two


class BrickShifts(Shifts):
    def __init__(self, shape):
        lane = lax.broadcasted_iota(jnp.int32, shape, 1)
        self.rows = shape[0]
        self.z = lane & 3
        self.odd = (lane >= 64, (lane & 4) != 0, (lane & 1) != 0)

    def y_moved(self, values, by):
        return self.lane_roll(values, -4 * by)

    def slab(self, values, by):
        return pltpu.roll(values, (-by) % self.rows, 0)

    def other(self, values):
        return self.lane_roll(values, 64)


class SlabShifts(Shifts):
    lane_axis = 2

    def __init__(self, shape):
        self.lane = lax.broadcasted_iota(jnp.int32, shape, 2)
        self.plane = lax.broadcasted_iota(jnp.int32, shape, 1) & 1
        self.z = self.lane & 3
        self.odd = (self.plane != 0, (self.lane & 4) != 0, (self.lane & 1) != 0)

    def y_moved(self, values, by):
        rolled = self.lane_roll(values, -4 * by)
        if by > 0:
            return jnp.where(
                self.lane < 128 - 4 * by, rolled, pltpu.roll(rolled, 6, 1)
            )
        return jnp.where(self.lane >= -4 * by, rolled, pltpu.roll(rolled, 2, 1))

    def slab(self, values, by):
        if by == 1:
            return jnp.concatenate([values[1:], values[:1]], 0)
        return jnp.concatenate([values[-1:], values[:-1]], 0)

    def other(self, values):
        return jnp.where(self.plane == 0, pltpu.roll(values, 7, 1), pltpu.roll(values, 1, 1))


def inverse_mass(shifts):
    odd_x, odd_y, odd_z = shifts.odd
    return (
        jnp.where(odd_x, 1.5, 3.0) * jnp.where(odd_y, 1.5, 3.0) * jnp.where(odd_z, 1.5, 3.0)
    )


def heat_step(field, heat, kappa, shifts):
    act = stiffness_action(kappa, shifts)
    inverse = inverse_mass(shifts)
    rate_one = (heat - act(field)) * inverse
    middle = field + STEP * rate_one
    rate_two = (heat - act(middle)) * inverse
    return field + (0.5 * STEP) * (rate_one + rate_two)


def blocks(values):
    return jnp.concatenate([values[:, 128 * q : 128 * q + 128] for q in range(4)], 0)


def lookup(table_ref, labels):
    low = labels & 127
    high = labels >> 8
    found = jnp.zeros(labels.shape, jnp.int32)
    for row in range(32):
        words = jnp.broadcast_to(table_ref[row : row + 1, :], labels.shape)
        found = jnp.where(high == row, take_lanes(words, low), found)
    return jnp.where((labels & 128) != 0, found >> 12, found & 4095)


def kernel(
    groups,
    slabs,
    field_ref,
    kappa_ref,
    heat_ref,
    solid_ref,
    label_ref,
    table_ref,
    slot_ref,
    seed_ref,
    matrix_ref,
    new_field_ref,
    new_solid_ref,
    outbox,
    inbox,
    near_field,
    near_heat,
    near_kappa,
    words,
    ahead_x,
    behind_x,
    ahead_y,
    behind_y,
    from_ahead_x,
    from_behind_x,
    from_ahead_y,
    from_behind_y,
    gathered,
    nucleation,
    planes,
    tally,
    box_sems,
    near_sems,
    near_send_sems,
    edge_recv_sems,
    edge_send_sems,
):
    g = lax.axis_index("grp")
    h = lax.axis_index("slab")
    g_next = lax.rem(g + 1, groups)
    g_prev = lax.rem(g + groups - 1, groups)
    high_edge = h >= slabs - 2
    low_edge = h <= 2

    barrier = pltpu.get_barrier_semaphore()

    def greet(to_g, to_h):
        pl.semaphore_signal(barrier, inc=1, device_id=(to_g, to_h), device_id_type=MESH)

    greet(g_prev, jnp.int32(slabs - 2))
    greet(g_prev, jnp.int32(slabs - 1))
    for first in range(3):
        greet(g_next, jnp.int32(first))
    greet(g_prev, h)
    greet(g_next, h)

    def greet_group(step, carry):
        greet(g, lax.rem(h + 1 + step, slabs))
        return carry

    lax.fori_loop(0, slabs - 1, greet_group, 0)

    sub = lax.broadcasted_iota(jnp.int32, (8, 128), 0)
    lane = lax.broadcasted_iota(jnp.int32, (8, 128), 1)
    window = 8 * sub + (lane & 63)
    even_lane = lane < 64
    kappa_lane = (lane >= 44) & (lane < 56)
    kappa_rows = jnp.broadcast_to(kappa_ref[...], (8, 128))
    shifted_field = [pltpu.roll(field_ref[...], 16, 1), pltpu.roll(field_ref[...], 512 - 48, 1)]
    shifted_heat = [pltpu.roll(heat_ref[...], 16, 1), pltpu.roll(heat_ref[...], 512 - 48, 1)]

    def windows(shifted, m):
        part = shifted[m % 2][:, 128 * (m // 2) : 128 * (m // 2) + 128]
        even = take_lanes(jnp.broadcast_to(part[0:1], (8, 128)), window)
        odd = take_lanes(jnp.broadcast_to(part[1:2], (8, 128)), window)
        return jnp.where(even_lane, even, odd)

    for m in range(slabs // 8):
        outbox[8 * m : 8 * m + 8, 0:128] = windows(shifted_field, m)
        index = (2 * (8 * m + sub) - 4 + lane - 44) & 127
        outbox[8 * m : 8 * m + 8, 128:256] = jnp.where(
            kappa_lane, take_lanes(kappa_rows, index), windows(shifted_heat, m)
        )

    expected = 63 + 2 + jnp.where(high_edge, slabs, 0) + jnp.where(low_edge, slabs, 0)
    pl.semaphore_wait(barrier, expected)

    def post(to_g, to_h, row):
        return pltpu.make_async_remote_copy(
            src_ref=outbox.at[pl.ds(to_h, 1), :],
            dst_ref=inbox.at[pl.ds(row, 1), :],
            send_sem=box_sems.at[0],
            recv_sem=box_sems.at[1],
            device_id=(to_g, to_h),
            device_id_type=MESH,
        )

    def wait_messages(many, kind):
        size = tally.at[pl.ds(0, many)]
        pltpu.make_async_copy(size, size, box_sems.at[kind]).wait()

    here = g * slabs + h
    count = groups * slabs
    near = []
    for by in (1, -1, 2, -2):
        there = lax.rem(here + by + count, count)
        device = (there // slabs, lax.rem(there, slabs))
        slot = {2: 0, 1: 1, -1: 2, -2: 3}[by]
        pairs = [(field_ref, near_field, slot, 0)]
        if by in (1, -1):
            pairs.append((heat_ref, near_heat, slot - 1, 1))
        if by != -2:
            pairs.append((kappa_ref, near_kappa, slot, 2))
        for source, target, place, kind in pairs:
            copy = pltpu.make_async_remote_copy(
                src_ref=source,
                dst_ref=target.at[place],
                send_sem=near_send_sems.at[slot, kind],
                recv_sem=near_sems.at[slot, kind],
                device_id=device,
                device_id_type=MESH,
            )
            copy.start()
            near.append(copy)

    def post_group(step, carry):
        to_h = lax.rem(h + 1 + step, slabs)
        post(g, to_h, h + 2).start()
        return carry

    @pl.when(high_edge)
    def _():
        def body(to_h, carry):
            post(g_next, to_h, h - (slabs - 2)).start()
            return carry

        lax.fori_loop(0, slabs, body, 0)

    @pl.when(low_edge)
    def _():
        def body(to_h, carry):
            post(g_prev, to_h, h + slabs + 2).start()
            return carry

        lax.fori_loop(0, slabs, body, 0)

    lax.fori_loop(0, slabs - 1, post_group, 0)

    weight = 1 << (2 * lax.broadcasted_iota(jnp.int32, (6, 1), 0))
    codes = jnp.sum((table_ref[...] - 1) * weight, axis=0, keepdims=True)
    words[...] = jnp.zeros(words.shape, jnp.int32)
    for row in range(31):
        low_half = codes[:, 256 * row : 256 * row + 128]
        high_half = codes[:, 256 * row + 128 : 256 * row + 256]
        words[row : row + 1, :] = low_half | (high_half << 12)
    words[31:32, 0:64] = codes[:, 7936:8000]

    lane_c = lax.broadcasted_iota(jnp.int32, (CHUNK, 128), 1)
    depth = lane_c & 15

    def cells(c, carry):
        rows = pl.ds(pl.multiple_of(c * CHUNK, CHUNK), CHUNK)
        code = lookup(words, label_ref[rows, :])
        quarter = 0.25 * solid_ref[rows, :]

        def weighted(d):
            return quarter * (((code >> (2 * d)) & 3) + 1).astype(jnp.float32)

        ahead_x[rows, :] = weighted(0)
        behind_x[rows, :] = weighted(1)
        up_y = weighted(2)
        down_y = weighted(3)
        up_z = weighted(4)
        down_z = weighted(5)
        gathered[rows, :] = (
            jnp.where(depth == 15, pltpu.roll(up_z, 15, 1), pltpu.roll(up_z, 127, 1))
            + jnp.where(depth == 0, pltpu.roll(down_z, 113, 1), pltpu.roll(down_z, 1, 1))
            + jnp.where(lane_c < 112, pltpu.roll(up_y, 112, 1), 0.0)
            + jnp.where(lane_c >= 16, pltpu.roll(down_y, 16, 1), 0.0)
        )
        mine = (lane_c >> 4) == c
        ahead_y[...] = jnp.where(mine, pltpu.roll(up_y, 16 * c, 1), ahead_y[...])
        behind_y[...] = jnp.where(
            mine, pltpu.roll(down_y, lax.rem(16 * c + 16, 128), 1), behind_y[...]
        )
        return carry

    ahead_y[...] = jnp.zeros(ahead_y.shape, jnp.float32)
    behind_y[...] = jnp.zeros(behind_y.shape, jnp.float32)
    edge_x = solid_ref.shape[0]
    lax.fori_loop(0, edge_x // CHUNK, cells, 0)

    total = jnp.zeros((edge_x, 128), jnp.float32)
    cell_row = lax.broadcasted_iota(jnp.int32, (edge_x, 128), 0)
    cell_lane = lax.broadcasted_iota(jnp.int32, (128, 128), 0)
    for part in range(2):
        slots = slot_ref[part : part + 1, :]
        code = lookup(words, jnp.broadcast_to(seed_ref[part : part + 1, :], (8, 128)))
        level = jnp.full((8, 128), 6, jnp.int32)
        for d in range(6):
            level = level + ((code >> (2 * d)) & 3)
        level = level[0:1].astype(jnp.float32)
        at_row = jnp.where(cell_row == (slots >> 7), 1.0, 0.0).astype(jnp.bfloat16)
        at_lane = jnp.where(cell_lane == (slots & 127), level, 0.0).astype(jnp.bfloat16)
        total = total + lax.dot_general(
            at_row, at_lane, (((1,), (1,)), ((), ())), preferred_element_type=jnp.float32
        )
    nucleation[...] = total * (1.0 / 6.0)

    h_next = lax.rem(h + 1, slabs)
    h_prev = lax.rem(h + slabs - 1, slabs)
    edges = []
    for number, (source, target, device) in enumerate(
        (
            (ahead_y, from_ahead_y, (g, h_prev)),
            (behind_y, from_behind_y, (g, h_next)),
            (ahead_x.at[0:8, :], from_ahead_x, (g_prev, h)),
            (behind_x.at[edge_x - 8 : edge_x, :], from_behind_x, (g_next, h)),
        )
    ):
        copy = pltpu.make_async_remote_copy(
            src_ref=source,
            dst_ref=target,
            send_sem=edge_send_sems.at[number],
            recv_sem=edge_recv_sems.at[number],
            device_id=device,
            device_id_type=MESH,
        )
        copy.start()
        edges.append(copy)

    gathered[0 : edge_x - 1, :] = gathered[0 : edge_x - 1, :] + ahead_x[1:edge_x, :]
    gathered[1:edge_x, :] = gathered[1:edge_x, :] + behind_x[0 : edge_x - 1, :]

    for copy in near:
        copy.wait_recv()
    zero = jnp.zeros((8, 128), jnp.float32)
    stacked_field = jnp.stack(
        [
            blocks(near_field[0]),
            blocks(near_field[1]),
            blocks(field_ref[...]),
            blocks(near_field[2]),
            blocks(near_field[3]),
        ],
        0,
    )
    stacked_heat = jnp.stack(
        [zero, blocks(near_heat[0]), blocks(heat_ref[...]), blocks(near_heat[1]), zero], 0
    )

    block_of = sub >> 1

    def expanded(row):
        index = block_of * 32 + (lane >> 3) * 2 + ((lane >> 1) & 1)
        return take_lanes(jnp.broadcast_to(row, (8, 128)), index)

    stacked_kappa = jnp.stack(
        [
            expanded(near_kappa[0]),
            expanded(near_kappa[1]),
            expanded(kappa_ref[...]),
            expanded(near_kappa[2]),
            zero,
        ],
        0,
    )
    moved = heat_step(
        stacked_field, stacked_heat, stacked_kappa, SlabShifts((5, 8, 128))
    )[2]
    for q in range(4):
        new_field_ref[:, 128 * q : 128 * q + 128] = moved[2 * q : 2 * q + 2, :]

    inbox[pl.ds(h + 2, 1), :] = outbox[pl.ds(h, 1), :]
    wait_messages(slabs + 4, 1)
    shifts = BrickShifts((ROWS, 128))
    box_lane = lax.broadcasted_iota(jnp.int32, (ROWS, 128), 1)
    half = box_lane & 63
    brick_heat = inbox[:, 128:256]
    brick_kappa = take_lanes(
        brick_heat, jnp.minimum(44 + (half >> 3) * 2 + ((half >> 1) & 1), 55)
    )
    brick = heat_step(inbox[:, 0:128], brick_heat, brick_kappa, shifts)
    box_row = lax.broadcasted_iota(jnp.int32, (ROWS, 128), 0)
    wanted = (half >= 16) & (half < 28) & (box_row >= 2) & (box_row < slabs + 3)
    brick = pltpu.roll(jnp.where(wanted, brick, 0.0), ROWS - 2, 0)
    pair = jnp.dot(
        brick, matrix_ref[...], precision=HIGHEST, preferred_element_type=jnp.float32
    )
    planes[:, 0:256] = pair
    planes[:, 256:384] = pltpu.roll(pair[:, 0:128], ROWS - 1, 0)

    for copy in edges:
        copy.wait_recv()
    gathered[edge_x - 1 : edge_x, :] = gathered[edge_x - 1 : edge_x, :] + from_ahead_x[0:1, :]
    gathered[0:1, :] = gathered[0:1, :] + from_behind_x[7:8, :]
    point = (sub.astype(jnp.float32) + 0.5) * 0.125
    basis = (
        2.0 * (point - 0.5) * (point - 1.0),
        -4.0 * point * (point - 1.0),
        2.0 * point * (point - 0.5),
    )

    def finish(c, carry):
        rows = pl.ds(pl.multiple_of(c * CHUNK, CHUNK), CHUNK)
        layer = planes[pl.ds(pl.multiple_of(c * (CHUNK // 8), CHUNK // 8), CHUNK // 8), :]
        parts = []
        for k in range(CHUNK // 8):
            parts.append(
                basis[0] * layer[k : k + 1, 0:128]
                + basis[1] * layer[k : k + 1, 128:256]
                + basis[2] * layer[k : k + 1, 256:384]
            )
        under = jnp.maximum(-jnp.concatenate(parts, 0), 0.0)
        side = jnp.where(
            lane_c >= 112,
            pltpu.roll(from_ahead_y[...], lax.rem(240 - 16 * c, 128), 1),
            jnp.where(
                lane_c < 16, pltpu.roll(from_behind_y[...], lax.rem(128 - 16 * c, 128), 1), 0.0
            ),
        )
        rate = under * (under * (gathered[rows, :] + side) + nucleation[rows, :])
        solid = solid_ref[rows, :]
        new_solid_ref[rows, :] = solid + (1.0 - solid) * (1.0 - jnp.exp(-rate))
        return carry

    lax.fori_loop(0, edge_x // CHUNK, finish, 0)

    for copy in near + edges:
        copy.wait_send()
    @pl.when(high_edge | low_edge)
    def _():
        wait_messages(2 * slabs - 1, 0)

    @pl.when(jnp.logical_not(high_edge | low_edge))
    def _():
        wait_messages(slabs - 1, 0)


def solution(mesh):
    groups, slabs = mesh.shape["grp"], mesh.shape["slab"]
    matrix = interpolation_matrix()

    def body(field, kappa, heat, solid, label, table, slot, seed):
        vmem = pl.BlockSpec(memory_space=pltpu.VMEM)
        edge_x = solid.shape[0]
        f32 = jnp.float32
        return pl.pallas_call(
            functools.partial(kernel, groups, slabs),
            out_shape=(
                jax.ShapeDtypeStruct(field.shape, f32),
                jax.ShapeDtypeStruct(solid.shape, f32),
            ),
            in_specs=[vmem] * 9,
            out_specs=(vmem, vmem),
            scratch_shapes=[
                pltpu.VMEM((slabs, 256), f32),
                pltpu.VMEM((ROWS, 256), f32),
                pltpu.VMEM((4, 2, 512), f32),
                pltpu.VMEM((2, 2, 512), f32),
                pltpu.VMEM((3, 1, 128), f32),
                pltpu.VMEM((32, 128), jnp.int32),
                pltpu.VMEM((edge_x, 128), f32),
                pltpu.VMEM((edge_x, 128), f32),
                pltpu.VMEM((CHUNK, 128), f32),
                pltpu.VMEM((CHUNK, 128), f32),
                pltpu.VMEM((8, 128), f32),
                pltpu.VMEM((8, 128), f32),
                pltpu.VMEM((CHUNK, 128), f32),
                pltpu.VMEM((CHUNK, 128), f32),
                pltpu.VMEM((edge_x, 128), f32),
                pltpu.VMEM((edge_x, 128), f32),
                pltpu.VMEM((ROWS, 384), f32),
                pltpu.VMEM((2 * slabs, 2, 128), f32),
                pltpu.SemaphoreType.DMA((2,)),
                pltpu.SemaphoreType.DMA((4, 3)),
                pltpu.SemaphoreType.DMA((4, 3)),
                pltpu.SemaphoreType.DMA((4,)),
                pltpu.SemaphoreType.DMA((4,)),
            ],
            compiler_params=pltpu.CompilerParams(collective_id=0, has_side_effects=True),
        )(
            field,
            kappa,
            heat,
            solid,
            label,
            table.T,
            slot.reshape(2, 128),
            seed.reshape(2, 128),
            jnp.asarray(matrix),
        )

    in_specs = (
        P(("grp", "slab"), None),
        P(("grp", "slab"), None),
        P(("grp", "slab"), None),
        P("grp", "slab"),
        P("grp", "slab"),
        P(),
        P(("grp", "slab")),
        P(("grp", "slab")),
    )
    out_specs = (P(("grp", "slab"), None), P("grp", "slab"))
    return jax.shard_map(body, mesh=mesh, in_specs=in_specs, out_specs=out_specs, check_vma=False)
```

```python
import functools

import jax
import jax.numpy as jnp
import numpy as np
from jax import lax
from jax.experimental import pallas as pl
from jax.experimental.pallas import tpu as pltpu
from jax.sharding import PartitionSpec as P

MESH = pl.DeviceIdType.MESH
HIGHEST = lax.Precision.HIGHEST
STEP = 0.004
CHUNK = 64
ROWS = 72


def interpolation_matrix():
    points = (np.arange(8) + 0.5) / 8
    basis = np.stack(
        [
            2.0 * (points - 0.5) * (points - 1.0),
            -4.0 * points * (points - 1.0),
            2.0 * points * (points - 0.5),
        ],
        1,
    )
    along_z = np.zeros((4, 16))
    for c in range(2):
        for p in range(8):
            for k in range(3):
                along_z[(2 * c + k) % 4, 8 * c + p] += basis[p, k]
    plane = np.einsum("nj,zc->jznc", basis, along_z).reshape(12, 128)
    matrix = np.zeros((128, 256), np.float32)
    matrix[16:28, :128] = plane
    matrix[80:92, 128:] = plane
    return matrix


def take_lanes(values, index):
    return jnp.take_along_axis(values, index, axis=1, mode="promise_in_bounds")


def stiffness_action(kappa, shifts):
    odd_x, odd_y, odd_z = shifts.odd

    def spread(values, axis):
        before = shifts.moved(values, axis, -1)
        return jnp.where(
            shifts.odd[axis], (2.0 / 3.0) * values, (1.0 / 6.0) * (values + before)
        )

    def spread_x(values):
        return jnp.where(
            odd_x,
            (2.0 / 3.0) * values,
            (1.0 / 6.0) * (values + shifts.slab(values, -1)),
        )

    over_x = spread_x(kappa)
    fields = (
        spread(spread(kappa, 1), 2) * (1.0 / 3.0),
        spread(over_x, 2) * (1.0 / 3.0),
        spread(over_x, 1) * (1.0 / 3.0),
    )
    centre = None
    pairs = []
    for axis in range(3):
        here = fields[axis]
        if axis == 0:
            before = shifts.slab(here, -1)
        else:
            before = shifts.moved(here, axis, -1)
        part = jnp.where(shifts.odd[axis], 16.0 * here, 7.0 * (here + before))
        centre = part if centre is None else centre + part
        pairs.append((here, jnp.where(shifts.odd[axis], here, before)))

    def act(values):
        total = centre * values
        for axis in range(3):
            ahead, behind = pairs[axis]
            one, two, back, back_two = shifts.neighbours(values, axis)
            odd = shifts.odd[axis]
            total = total + ahead * (jnp.where(odd, 0.0, two) - 8.0 * one)
            total = total + behind * (jnp.where(odd, 0.0, back_two) - 8.0 * back)
        return total

    return act


class Shifts:
    lane_axis = 1

    def lane_roll(self, values, by):
        return pltpu.roll(values, by % 128, self.lane_axis)

    def z_moved(self, values, by):
        z = self.z
        if by == 1:
            return jnp.where(z == 3, self.lane_roll(values, 3), self.lane_roll(values, -1))
        if by == -1:
            return jnp.where(z == 0, self.lane_roll(values, -3), self.lane_roll(values, 1))
        return jnp.where(z >= 2, self.lane_roll(values, 2), self.lane_roll(values, -2))

    def moved(self, values, axis, by):
        if axis == 1:
            return self.y_moved(values, by)
        return self.z_moved(values, by)

    def neighbours(self, values, axis):
        if axis == 0:
            other = self.other(values)
            ahead = jnp.where(self.odd[0], self.slab(other, 1), other)
            behind = jnp.where(self.odd[0], other, self.slab(other, -1))
            return ahead, self.slab(values, 1), behind, self.slab(values, -1)
        if axis == 1:
            return tuple(self.y_moved(values, by) for by in (1, 2, -1, -2))
        two = self.z_moved(values, 2)
        return self.z_moved(values, 1), two, self.z_moved(values, -1), two


class BrickShifts(Shifts):
    def __init__(self, shape):
        lane = lax.broadcasted_iota(jnp.int32, shape, 1)
        self.rows = shape[0]
        self.z = lane & 3
        self.odd = (lane >= 64, (lane & 4) != 0, (lane & 1) != 0)

    def y_moved(self, values, by):
        return self.lane_roll(values, -4 * by)

    def slab(self, values, by):
        return pltpu.roll(values, (-by) % self.rows, 0)

    def other(self, values):
        return self.lane_roll(values, 64)


class SlabShifts(Shifts):
    lane_axis = 2

    def __init__(self, shape):
        self.lane = lax.broadcasted_iota(jnp.int32, shape, 2)
        self.plane = lax.broadcasted_iota(jnp.int32, shape, 1) & 1
        self.z = self.lane & 3
        self.odd = (self.plane != 0, (self.lane & 4) != 0, (self.lane & 1) != 0)

    def y_moved(self, values, by):
        rolled = self.lane_roll(values, -4 * by)
        if by > 0:
            return jnp.where(
                self.lane < 128 - 4 * by, rolled, pltpu.roll(rolled, 6, 1)
            )
        return jnp.where(self.lane >= -4 * by, rolled, pltpu.roll(rolled, 2, 1))

    def slab(self, values, by):
        if by == 1:
            return jnp.concatenate([values[1:], values[:1]], 0)
        return jnp.concatenate([values[-1:], values[:-1]], 0)

    def other(self, values):
        return jnp.where(self.plane == 0, pltpu.roll(values, 7, 1), pltpu.roll(values, 1, 1))


def inverse_mass(shifts):
    odd_x, odd_y, odd_z = shifts.odd
    return (
        jnp.where(odd_x, 1.5, 3.0) * jnp.where(odd_y, 1.5, 3.0) * jnp.where(odd_z, 1.5, 3.0)
    )


def heat_step(field, heat, kappa, shifts):
    act = stiffness_action(kappa, shifts)
    inverse = inverse_mass(shifts)
    rate_one = (heat - act(field)) * inverse
    middle = field + STEP * rate_one
    rate_two = (heat - act(middle)) * inverse
    return field + (0.5 * STEP) * (rate_one + rate_two)


def blocks(values):
    return jnp.concatenate([values[:, 128 * q : 128 * q + 128] for q in range(4)], 0)


def lookup(table_ref, labels):
    low = labels & 127
    bits = [(labels & (256 << level)) != 0 for level in range(5)]

    def choose(first, level):
        if level < 0:
            return take_lanes(table_ref[8 * first : 8 * first + 8, :], low)
        return jnp.where(
            bits[level], choose(first + (1 << level), level - 1), choose(first, level - 1)
        )

    found = choose(0, 4)
    return jnp.where((labels & 128) != 0, found >> 12, found & 4095)


def exchange(
    groups,
    slabs,
    field_any,
    kappa_any,
    heat_any,
    solid_any,
    label_any,
    table_any,
    slot_any,
    seed_any,
    matrix_any,
    new_field_ref,
    solid_ref,
    planes,
    gathered,
    nucleation,
    side_ahead,
    side_behind,
    field_ref,
    kappa_ref,
    heat_ref,
    label_ref,
    table_ref,
    slot_ref,
    seed_ref,
    matrix_ref,
    outbox,
    inbox,
    near_field,
    near_heat,
    near_kappa,
    words,
    ahead_x,
    behind_x,
    ahead_y,
    behind_y,
    from_ahead_x,
    from_behind_x,
    from_ahead_y,
    from_behind_y,
    tally,
    load_sems,
    box_sems,
    near_sems,
    near_send_sems,
    edge_recv_sems,
    edge_send_sems,
):
    loads = []
    for number, (source, target) in enumerate(
        (
            (field_any, field_ref),
            (heat_any, heat_ref),
            (kappa_any, kappa_ref),
            (table_any, table_ref),
            (label_any, label_ref),
            (solid_any, solid_ref),
            (slot_any, slot_ref),
            (seed_any, seed_ref),
            (matrix_any, matrix_ref),
        )
    ):
        copy = pltpu.make_async_copy(source, target, load_sems.at[number])
        copy.start()
        loads.append(copy)
    g = lax.axis_index("grp")
    h = lax.axis_index("slab")
    g_next = lax.rem(g + 1, groups)
    g_prev = lax.rem(g + groups - 1, groups)
    high_edge = h >= slabs - 2
    low_edge = h <= 2

    barrier = pltpu.get_barrier_semaphore()

    def greet(to_g, to_h):
        pl.semaphore_signal(barrier, inc=1, device_id=(to_g, to_h), device_id_type=MESH)

    greet(g_prev, jnp.int32(slabs - 2))
    greet(g_prev, jnp.int32(slabs - 1))
    for first in range(3):
        greet(g_next, jnp.int32(first))
    greet(g_prev, h)
    greet(g_next, h)

    def greet_group(step, carry):
        greet(g, lax.rem(h + 1 + step, slabs))
        return carry

    lax.fori_loop(0, slabs - 1, greet_group, 0)

    for copy in loads[:3]:
        copy.wait()
    sub = lax.broadcasted_iota(jnp.int32, (8, 128), 0)
    lane = lax.broadcasted_iota(jnp.int32, (8, 128), 1)
    window = 8 * sub + (lane & 63)
    even_lane = lane < 64
    kappa_lane = (lane >= 44) & (lane < 56)
    kappa_rows = jnp.broadcast_to(kappa_ref[...], (8, 128))
    shifted_field = [pltpu.roll(field_ref[...], 16, 1), pltpu.roll(field_ref[...], 512 - 48, 1)]
    shifted_heat = [pltpu.roll(heat_ref[...], 16, 1), pltpu.roll(heat_ref[...], 512 - 48, 1)]

    def windows(shifted, m):
        part = shifted[m % 2][:, 128 * (m // 2) : 128 * (m // 2) + 128]
        even = take_lanes(jnp.broadcast_to(part[0:1], (8, 128)), window)
        odd = take_lanes(jnp.broadcast_to(part[1:2], (8, 128)), window)
        return jnp.where(even_lane, even, odd)

    for m in range(slabs // 8):
        outbox[8 * m : 8 * m + 8, 0:128] = windows(shifted_field, m)
        index = (2 * (8 * m + sub) - 4 + lane - 44) & 127
        outbox[8 * m : 8 * m + 8, 128:256] = jnp.where(
            kappa_lane, take_lanes(kappa_rows, index), windows(shifted_heat, m)
        )

    for copy in loads[3:]:
        copy.wait()
    weight = 1 << (2 * lax.broadcasted_iota(jnp.int32, (6, 1), 0))
    codes = jnp.sum((table_ref[...] - 1) * weight, axis=0, keepdims=True)
    for row in range(31):
        low_half = codes[:, 256 * row : 256 * row + 128]
        high_half = codes[:, 256 * row + 128 : 256 * row + 256]
        words[8 * row : 8 * row + 8, :] = jnp.broadcast_to(
            low_half | (high_half << 12), (8, 128)
        )
    rest = jnp.concatenate([codes[:, 7936:8000], jnp.zeros((1, 64), jnp.int32)], 1)
    words[248:256, :] = jnp.broadcast_to(rest, (8, 128))

    lane_c = lax.broadcasted_iota(jnp.int32, (CHUNK, 128), 1)
    depth = lane_c & 15

    def cells(c, carry):
        rows = pl.ds(pl.multiple_of(c * CHUNK, CHUNK), CHUNK)
        labels = label_ref[rows, :]
        code = jnp.concatenate(
            [lookup(words, labels[8 * k : 8 * k + 8]) for k in range(CHUNK // 8)], 0
        )
        quarter = 0.25 * solid_ref[rows, :]

        def weighted(d):
            return quarter * (((code >> (2 * d)) & 3) + 1).astype(jnp.float32)

        ahead_x[rows, :] = weighted(0)
        behind_x[rows, :] = weighted(1)
        up_y = weighted(2)
        down_y = weighted(3)
        up_z = weighted(4)
        down_z = weighted(5)
        gathered[rows, :] = (
            jnp.where(depth == 15, pltpu.roll(up_z, 15, 1), pltpu.roll(up_z, 127, 1))
            + jnp.where(depth == 0, pltpu.roll(down_z, 113, 1), pltpu.roll(down_z, 1, 1))
            + jnp.where(lane_c < 112, pltpu.roll(up_y, 112, 1), 0.0)
            + jnp.where(lane_c >= 16, pltpu.roll(down_y, 16, 1), 0.0)
        )
        mine = (lane_c >> 4) == c
        ahead_y[...] = jnp.where(mine, pltpu.roll(up_y, 16 * c, 1), ahead_y[...])
        behind_y[...] = jnp.where(
            mine, pltpu.roll(down_y, lax.rem(16 * c + 16, 128), 1), behind_y[...]
        )
        return carry

    ahead_y[...] = jnp.zeros(ahead_y.shape, jnp.float32)
    behind_y[...] = jnp.zeros(behind_y.shape, jnp.float32)
    edge_x = solid_ref.shape[0]
    chunks = edge_x // CHUNK
    x, y = lax.rem(h // 2, 4), h // 8
    hops = jnp.abs(x - 2) + jnp.abs(y - 4)
    ahead = jnp.where(g == 0, chunks, jnp.minimum(2 * hops, chunks))
    lax.fori_loop(0, ahead, cells, 0)

    expected = 63 + 2 + jnp.where(high_edge, slabs, 0) + jnp.where(low_edge, slabs, 0)
    pl.semaphore_wait(barrier, expected)

    def post(to_g, to_h, row):
        return pltpu.make_async_remote_copy(
            src_ref=outbox.at[pl.ds(to_h, 1), :],
            dst_ref=inbox.at[pl.ds(row, 1), :],
            send_sem=box_sems.at[0],
            recv_sem=box_sems.at[1],
            device_id=(to_g, to_h),
            device_id_type=MESH,
        )

    def wait_messages(many, kind):
        size = tally.at[pl.ds(0, many)]
        pltpu.make_async_copy(size, size, box_sems.at[kind]).wait()

    here = g * slabs + h
    count = groups * slabs
    near = []
    for by in (1, -1, 2, -2):
        there = lax.rem(here + by + count, count)
        device = (there // slabs, lax.rem(there, slabs))
        slot = {2: 0, 1: 1, -1: 2, -2: 3}[by]
        pairs = [(field_ref, near_field, slot, 0)]
        if by in (1, -1):
            pairs.append((heat_ref, near_heat, slot - 1, 1))
        if by != -2:
            pairs.append((kappa_ref, near_kappa, slot, 2))
        for source, target, place, kind in pairs:
            copy = pltpu.make_async_remote_copy(
                src_ref=source,
                dst_ref=target.at[place],
                send_sem=near_send_sems.at[slot, kind],
                recv_sem=near_sems.at[slot, kind],
                device_id=device,
                device_id_type=MESH,
            )
            copy.start()
            near.append(copy)

    def post_group(step, carry):
        to_h = lax.rem(h + 1 + step, slabs)
        post(g, to_h, h + 2).start()
        return carry

    @pl.when(high_edge)
    def _():
        def body(to_h, carry):
            post(g_next, to_h, h - (slabs - 2)).start()
            return carry

        lax.fori_loop(0, slabs, body, 0)

    @pl.when(low_edge)
    def _():
        def body(to_h, carry):
            post(g_prev, to_h, h + slabs + 2).start()
            return carry

        lax.fori_loop(0, slabs, body, 0)

    lax.fori_loop(0, slabs - 1, post_group, 0)

    lax.fori_loop(ahead, chunks, cells, 0)

    total = jnp.zeros((edge_x, 128), jnp.float32)
    cell_row = lax.broadcasted_iota(jnp.int32, (edge_x, 128), 0)
    cell_lane = lax.broadcasted_iota(jnp.int32, (128, 128), 0)
    for part in range(2):
        slots = slot_ref[part : part + 1, :]
        code = lookup(words, jnp.broadcast_to(seed_ref[part : part + 1, :], (8, 128)))
        level = jnp.full((8, 128), 6, jnp.int32)
        for d in range(6):
            level = level + ((code >> (2 * d)) & 3)
        level = level[0:1].astype(jnp.float32)
        at_row = jnp.where(cell_row == (slots >> 7), 1.0, 0.0).astype(jnp.bfloat16)
        at_lane = jnp.where(cell_lane == (slots & 127), level, 0.0).astype(jnp.bfloat16)
        total = total + lax.dot_general(
            at_row, at_lane, (((1,), (1,)), ((), ())), preferred_element_type=jnp.float32
        )
    nucleation[...] = total * (1.0 / 6.0)

    h_next = lax.rem(h + 1, slabs)
    h_prev = lax.rem(h + slabs - 1, slabs)
    edges = []
    for number, (source, target, device) in enumerate(
        (
            (ahead_y, from_ahead_y, (g, h_prev)),
            (behind_y, from_behind_y, (g, h_next)),
            (ahead_x.at[0:8, :], from_ahead_x, (g_prev, h)),
            (behind_x.at[edge_x - 8 : edge_x, :], from_behind_x, (g_next, h)),
        )
    ):
        copy = pltpu.make_async_remote_copy(
            src_ref=source,
            dst_ref=target,
            send_sem=edge_send_sems.at[number],
            recv_sem=edge_recv_sems.at[number],
            device_id=device,
            device_id_type=MESH,
        )
        copy.start()
        edges.append(copy)

    gathered[0 : edge_x - 1, :] = gathered[0 : edge_x - 1, :] + ahead_x[1:edge_x, :]
    gathered[1:edge_x, :] = gathered[1:edge_x, :] + behind_x[0 : edge_x - 1, :]

    for copy in near:
        copy.wait_recv()
    zero = jnp.zeros((8, 128), jnp.float32)
    stacked_field = jnp.stack(
        [
            blocks(near_field[0]),
            blocks(near_field[1]),
            blocks(field_ref[...]),
            blocks(near_field[2]),
            blocks(near_field[3]),
        ],
        0,
    )
    stacked_heat = jnp.stack(
        [zero, blocks(near_heat[0]), blocks(heat_ref[...]), blocks(near_heat[1]), zero], 0
    )

    block_of = sub >> 1

    def expanded(row):
        index = block_of * 32 + (lane >> 3) * 2 + ((lane >> 1) & 1)
        return take_lanes(jnp.broadcast_to(row, (8, 128)), index)

    stacked_kappa = jnp.stack(
        [
            expanded(near_kappa[0]),
            expanded(near_kappa[1]),
            expanded(kappa_ref[...]),
            expanded(near_kappa[2]),
            zero,
        ],
        0,
    )
    moved = heat_step(
        stacked_field, stacked_heat, stacked_kappa, SlabShifts((5, 8, 128))
    )[2]
    for q in range(4):
        new_field_ref[:, 128 * q : 128 * q + 128] = moved[2 * q : 2 * q + 2, :]

    inbox[pl.ds(h + 2, 1), :] = outbox[pl.ds(h, 1), :]
    wait_messages(slabs + 4, 1)
    shifts = BrickShifts((ROWS, 128))
    box_lane = lax.broadcasted_iota(jnp.int32, (ROWS, 128), 1)
    half = box_lane & 63
    brick_heat = inbox[:, 128:256]
    brick_kappa = take_lanes(
        brick_heat, jnp.minimum(44 + (half >> 3) * 2 + ((half >> 1) & 1), 55)
    )
    brick = heat_step(inbox[:, 0:128], brick_heat, brick_kappa, shifts)
    box_row = lax.broadcasted_iota(jnp.int32, (ROWS, 128), 0)
    wanted = (half >= 16) & (half < 28) & (box_row >= 2) & (box_row < slabs + 3)
    brick = pltpu.roll(jnp.where(wanted, brick, 0.0), ROWS - 2, 0)
    pair = jnp.dot(
        brick, matrix_ref[...], precision=HIGHEST, preferred_element_type=jnp.float32
    )
    planes[:, 0:256] = pair
    planes[:, 256:384] = pltpu.roll(pair[:, 0:128], ROWS - 1, 0)

    for copy in edges:
        copy.wait_recv()
    gathered[edge_x - 1 : edge_x, :] = gathered[edge_x - 1 : edge_x, :] + from_ahead_x[0:1, :]
    gathered[0:1, :] = gathered[0:1, :] + from_behind_x[7:8, :]
    side_ahead[...] = from_ahead_y[...]
    side_behind[...] = from_behind_y[...]

    for copy in near + edges:
        copy.wait_send()
    @pl.when(high_edge | low_edge)
    def _():
        wait_messages(2 * slabs - 1, 0)

    @pl.when(jnp.logical_not(high_edge | low_edge))
    def _():
        wait_messages(slabs - 1, 0)


def finish(
    field_ref,
    solid_ref,
    planes,
    gathered,
    nucleation,
    side_ahead,
    side_behind,
    new_field_any,
    new_solid_any,
    result,
    sems,
):
    chunks = solid_ref.shape[0] // CHUNK
    field_out = pltpu.make_async_copy(field_ref, new_field_any, sems.at[chunks])
    field_out.start()
    sub = lax.broadcasted_iota(jnp.int32, (8, 128), 0)
    lane_c = lax.broadcasted_iota(jnp.int32, (CHUNK, 128), 1)
    point = (sub.astype(jnp.float32) + 0.5) * 0.125
    basis = (
        2.0 * (point - 0.5) * (point - 1.0),
        -4.0 * point * (point - 1.0),
        2.0 * point * (point - 0.5),
    )
    stores = []
    for c in range(chunks):
        rows = slice(c * CHUNK, (c + 1) * CHUNK)
        layer = planes[c * (CHUNK // 8) : (c + 1) * (CHUNK // 8), :]
        parts = []
        for k in range(CHUNK // 8):
            parts.append(
                basis[0] * layer[k : k + 1, 0:128]
                + basis[1] * layer[k : k + 1, 128:256]
                + basis[2] * layer[k : k + 1, 256:384]
            )
        under = jnp.maximum(-jnp.concatenate(parts, 0), 0.0)
        side = jnp.where(
            lane_c >= 112,
            pltpu.roll(side_ahead[...], (240 - 16 * c) % 128, 1),
            jnp.where(lane_c < 16, pltpu.roll(side_behind[...], (128 - 16 * c) % 128, 1), 0.0),
        )
        rate = under * (under * (gathered[rows, :] + side) + nucleation[rows, :])
        solid = solid_ref[rows, :]
        result[rows, :] = solid + (1.0 - solid) * (1.0 - jnp.exp(-rate))
        copy = pltpu.make_async_copy(result.at[rows, :], new_solid_any.at[rows, :], sems.at[c])
        copy.start()
        stores.append(copy)
    for copy in stores:
        copy.wait()
    field_out.wait()


def solution(mesh):
    groups, slabs = mesh.shape["grp"], mesh.shape["slab"]
    matrix = interpolation_matrix()

    def body(field, kappa, heat, solid, label, table, slot, seed):
        vmem = pl.BlockSpec(memory_space=pltpu.VMEM)
        anywhere = pl.BlockSpec(memory_space=pl.ANY)
        edge_x = solid.shape[0]
        f32, i32 = jnp.float32, jnp.int32
        cells = (edge_x, 128)
        found = pl.pallas_call(
            functools.partial(exchange, groups, slabs),
            out_shape=(
                jax.ShapeDtypeStruct(field.shape, f32),
                jax.ShapeDtypeStruct(cells, f32),
                jax.ShapeDtypeStruct((ROWS, 384), f32),
                jax.ShapeDtypeStruct(cells, f32),
                jax.ShapeDtypeStruct(cells, f32),
                jax.ShapeDtypeStruct((CHUNK, 128), f32),
                jax.ShapeDtypeStruct((CHUNK, 128), f32),
            ),
            in_specs=[anywhere] * 9,
            out_specs=(vmem,) * 7,
            scratch_shapes=[
                pltpu.VMEM(field.shape, f32),
                pltpu.VMEM(kappa.shape, f32),
                pltpu.VMEM(heat.shape, f32),
                pltpu.VMEM(cells, i32),
                pltpu.VMEM(table.shape[::-1], i32),
                pltpu.VMEM((2, 128), i32),
                pltpu.VMEM((2, 128), i32),
                pltpu.VMEM(matrix.shape, f32),
                pltpu.VMEM((slabs, 256), f32),
                pltpu.VMEM((ROWS, 256), f32),
                pltpu.VMEM((4, 2, 512), f32),
                pltpu.VMEM((2, 2, 512), f32),
                pltpu.VMEM((3, 1, 128), f32),
                pltpu.VMEM((256, 128), i32),
                pltpu.VMEM(cells, f32),
                pltpu.VMEM(cells, f32),
                pltpu.VMEM((CHUNK, 128), f32),
                pltpu.VMEM((CHUNK, 128), f32),
                pltpu.VMEM((8, 128), f32),
                pltpu.VMEM((8, 128), f32),
                pltpu.VMEM((CHUNK, 128), f32),
                pltpu.VMEM((CHUNK, 128), f32),
                pltpu.VMEM((2 * slabs, 2, 128), f32),
                pltpu.SemaphoreType.DMA((9,)),
                pltpu.SemaphoreType.DMA((2,)),
                pltpu.SemaphoreType.DMA((4, 3)),
                pltpu.SemaphoreType.DMA((4, 3)),
                pltpu.SemaphoreType.DMA((4,)),
                pltpu.SemaphoreType.DMA((4,)),
            ],
            compiler_params=pltpu.CompilerParams(collective_id=0, has_side_effects=True),
        )(
            field,
            kappa,
            heat,
            solid,
            label,
            table.T,
            slot.reshape(2, 128),
            seed.reshape(2, 128),
            jnp.asarray(matrix),
        )
        return pl.pallas_call(
            finish,
            out_shape=(
                jax.ShapeDtypeStruct(field.shape, f32),
                jax.ShapeDtypeStruct(solid.shape, f32),
            ),
            in_specs=[vmem] * 7,
            out_specs=(anywhere, anywhere),
            scratch_shapes=[
                pltpu.VMEM(cells, f32),
                pltpu.SemaphoreType.DMA((edge_x // CHUNK + 1,)),
            ],
        )(*found)

    in_specs = (
        P(("grp", "slab"), None),
        P(("grp", "slab"), None),
        P(("grp", "slab"), None),
        P("grp", "slab"),
        P("grp", "slab"),
        P(),
        P(("grp", "slab")),
        P(("grp", "slab")),
    )
    out_specs = (P(("grp", "slab"), None), P("grp", "slab"))
    return jax.shard_map(body, mesh=mesh, in_specs=in_specs, out_specs=out_specs, check_vma=False)
```

```python
import functools

import jax
import jax.numpy as jnp
import numpy as np
from jax import lax
from jax.experimental import pallas as pl
from jax.experimental.pallas import tpu as pltpu
from jax.sharding import PartitionSpec as P

MESH = pl.DeviceIdType.MESH
HIGHEST = lax.Precision.HIGHEST
STEP = 0.004
CHUNK = 64
ROWS = 72


def interpolation_matrix():
    points = (np.arange(8) + 0.5) / 8
    basis = np.stack(
        [
            2.0 * (points - 0.5) * (points - 1.0),
            -4.0 * points * (points - 1.0),
            2.0 * points * (points - 0.5),
        ],
        1,
    )
    along_z = np.zeros((4, 16))
    for c in range(2):
        for p in range(8):
            for k in range(3):
                along_z[(2 * c + k) % 4, 8 * c + p] += basis[p, k]
    plane = np.einsum("nj,zc->jznc", basis, along_z).reshape(12, 128)
    matrix = np.zeros((128, 256), np.float32)
    matrix[16:28, :128] = plane
    matrix[80:92, 128:] = plane
    return matrix


def take_lanes(values, index):
    return jnp.take_along_axis(values, index, axis=1, mode="promise_in_bounds")


def stiffness_action(kappa, shifts):
    odd_x, odd_y, odd_z = shifts.odd

    def spread(values, axis):
        before = shifts.moved(values, axis, -1)
        return jnp.where(
            shifts.odd[axis], (2.0 / 3.0) * values, (1.0 / 6.0) * (values + before)
        )

    def spread_x(values):
        return jnp.where(
            odd_x,
            (2.0 / 3.0) * values,
            (1.0 / 6.0) * (values + shifts.slab(values, -1)),
        )

    over_x = spread_x(kappa)
    fields = (
        spread(spread(kappa, 1), 2) * (1.0 / 3.0),
        spread(over_x, 2) * (1.0 / 3.0),
        spread(over_x, 1) * (1.0 / 3.0),
    )
    centre = None
    pairs = []
    for axis in range(3):
        here = fields[axis]
        if axis == 0:
            before = shifts.slab(here, -1)
        else:
            before = shifts.moved(here, axis, -1)
        part = jnp.where(shifts.odd[axis], 16.0 * here, 7.0 * (here + before))
        centre = part if centre is None else centre + part
        pairs.append((here, jnp.where(shifts.odd[axis], here, before)))

    def act(values):
        total = centre * values
        for axis in range(3):
            ahead, behind = pairs[axis]
            one, two, back, back_two = shifts.neighbours(values, axis)
            odd = shifts.odd[axis]
            total = total + ahead * (jnp.where(odd, 0.0, two) - 8.0 * one)
            total = total + behind * (jnp.where(odd, 0.0, back_two) - 8.0 * back)
        return total

    return act


class Shifts:
    lane_axis = 1

    def lane_roll(self, values, by):
        return pltpu.roll(values, by % 128, self.lane_axis)

    def z_moved(self, values, by):
        z = self.z
        if by == 1:
            return jnp.where(z == 3, self.lane_roll(values, 3), self.lane_roll(values, -1))
        if by == -1:
            return jnp.where(z == 0, self.lane_roll(values, -3), self.lane_roll(values, 1))
        return jnp.where(z >= 2, self.lane_roll(values, 2), self.lane_roll(values, -2))

    def moved(self, values, axis, by):
        if axis == 1:
            return self.y_moved(values, by)
        return self.z_moved(values, by)

    def neighbours(self, values, axis):
        if axis == 0:
            other = self.other(values)
            ahead = jnp.where(self.odd[0], self.slab(other, 1), other)
            behind = jnp.where(self.odd[0], other, self.slab(other, -1))
            return ahead, self.slab(values, 1), behind, self.slab(values, -1)
        if axis == 1:
            return tuple(self.y_moved(values, by) for by in (1, 2, -1, -2))
        two = self.z_moved(values, 2)
        return self.z_moved(values, 1), two, self.z_moved(values, -1), two


class BrickShifts(Shifts):
    def __init__(self, shape):
        lane = lax.broadcasted_iota(jnp.int32, shape, 1)
        self.rows = shape[0]
        self.z = lane & 3
        self.odd = (lane >= 64, (lane & 4) != 0, (lane & 1) != 0)

    def y_moved(self, values, by):
        return self.lane_roll(values, -4 * by)

    def slab(self, values, by):
        return pltpu.roll(values, (-by) % self.rows, 0)

    def other(self, values):
        return self.lane_roll(values, 64)


class SlabShifts(Shifts):
    lane_axis = 2

    def __init__(self, shape):
        self.lane = lax.broadcasted_iota(jnp.int32, shape, 2)
        self.plane = lax.broadcasted_iota(jnp.int32, shape, 1) & 1
        self.z = self.lane & 3
        self.odd = (self.plane != 0, (self.lane & 4) != 0, (self.lane & 1) != 0)

    def y_moved(self, values, by):
        rolled = self.lane_roll(values, -4 * by)
        if by > 0:
            return jnp.where(
                self.lane < 128 - 4 * by, rolled, pltpu.roll(rolled, 6, 1)
            )
        return jnp.where(self.lane >= -4 * by, rolled, pltpu.roll(rolled, 2, 1))

    def slab(self, values, by):
        if by == 1:
            return jnp.concatenate([values[1:], values[:1]], 0)
        return jnp.concatenate([values[-1:], values[:-1]], 0)

    def other(self, values):
        return jnp.where(self.plane == 0, pltpu.roll(values, 7, 1), pltpu.roll(values, 1, 1))


def inverse_mass(shifts):
    odd_x, odd_y, odd_z = shifts.odd
    return (
        jnp.where(odd_x, 1.5, 3.0) * jnp.where(odd_y, 1.5, 3.0) * jnp.where(odd_z, 1.5, 3.0)
    )


def heat_step(field, heat, kappa, shifts):
    act = stiffness_action(kappa, shifts)
    inverse = inverse_mass(shifts)
    rate_one = (heat - act(field)) * inverse
    middle = field + STEP * rate_one
    rate_two = (heat - act(middle)) * inverse
    return field + (0.5 * STEP) * (rate_one + rate_two)


def blocks(values):
    return jnp.concatenate([values[:, 128 * q : 128 * q + 128] for q in range(4)], 0)


def lookup(table_ref, labels):
    low = labels & 127
    bits = [(labels & (256 << level)) != 0 for level in range(5)]

    def choose(first, level):
        if level < 0:
            return take_lanes(table_ref[8 * first : 8 * first + 8, :], low)
        return jnp.where(
            bits[level], choose(first + (1 << level), level - 1), choose(first, level - 1)
        )

    found = choose(0, 4)
    return jnp.where((labels & 128) != 0, found >> 12, found & 4095)


def exchange(
    groups,
    slabs,
    field_any,
    kappa_any,
    heat_any,
    solid_any,
    label_any,
    table_any,
    slot_any,
    seed_any,
    matrix_any,
    new_field_ref,
    solid_ref,
    planes,
    gathered,
    nucleation,
    side_ahead,
    side_behind,
    field_ref,
    kappa_ref,
    heat_ref,
    label_ref,
    table_ref,
    slot_ref,
    seed_ref,
    matrix_ref,
    outbox,
    inbox,
    near_field,
    near_heat,
    near_kappa,
    words,
    ahead_x,
    behind_x,
    ahead_y,
    behind_y,
    from_ahead_x,
    from_behind_x,
    from_ahead_y,
    from_behind_y,
    tally,
    edge_low,
    edge_high,
    load_sems,
    box_sems,
    row_sems,
    forward_sems,
    ready_sem,
    near_sems,
    near_send_sems,
    edge_recv_sems,
    edge_send_sems,
):
    loads = []
    for number, (source, target) in enumerate(
        (
            (field_any, field_ref),
            (heat_any, heat_ref),
            (kappa_any, kappa_ref),
            (table_any, table_ref),
            (label_any, label_ref),
            (solid_any, solid_ref),
            (slot_any, slot_ref),
            (seed_any, seed_ref),
            (matrix_any, matrix_ref),
        )
    ):
        copy = pltpu.make_async_copy(source, target, load_sems.at[number])
        copy.start()
        loads.append(copy)
    g = lax.axis_index("grp")
    h = lax.axis_index("slab")
    g_next = lax.rem(g + 1, groups)
    g_prev = lax.rem(g + groups - 1, groups)

    ordered = g == groups - 1

    def place(rank):
        fold = rank >> 3
        row = jnp.where((fold & 1) == 1, (fold + 1) >> 1, (0 - (fold >> 1)) & (slabs // 8 - 1))
        return 8 * row + (rank & 7)

    def rank_of(other):
        row = other >> 3
        fold = jnp.where(
            row == 0, 0, jnp.where(row <= slabs // 16, 2 * row - 1, slabs // 4 - 2 * row)
        )
        return 8 * fold + (other & 7)

    rank = rank_of(h)
    prev_upper = g == 0
    at_low, at_high = h <= 2, h >= slabs - 2
    sends_low = at_low & (g > 0) & jnp.logical_not(ordered)
    sends_high = at_high

    barrier = pltpu.get_barrier_semaphore()

    def greet(to_g, to_h):
        pl.semaphore_signal(barrier, inc=1, device_id=(to_g, to_h), device_id_type=MESH)

    greet(g_prev, h)
    for last in range(2):
        greet(g_prev, jnp.int32(slabs - 1 - last))

    @pl.when(jnp.logical_not(ordered))
    def _():
        greet(g_next, h)

    @pl.when(g < groups - 2)
    def _():
        for first in range(3):
            greet(g_next, jnp.int32(first))

    here = g * slabs + h
    count = groups * slabs
    near_to = {}
    for by in (1, -1, 2, -2):
        there = lax.rem(here + by + count, count)
        to_g, to_h = there // slabs, lax.rem(there, slabs)
        inside = to_g == g
        upper = jnp.where(
            inside, ordered & (rank_of(to_h) > rank), prev_upper if by < 0 else False
        )
        silent = ordered if by > 0 else False

        @pl.when(jnp.logical_not(inside | silent))
        def _(to_g=to_g, to_h=to_h):
            greet(to_g, to_h)

        near_to[by] = (to_g, to_h, inside, upper)

    def greet_rank(r, carry):
        greet(g, place(r))
        return carry

    lax.fori_loop(0, jnp.where(ordered, 0, rank), greet_rank, 0)
    lax.fori_loop(rank + 1, slabs, greet_rank, 0)

    for copy in loads[:3]:
        copy.wait()
    sub = lax.broadcasted_iota(jnp.int32, (8, 128), 0)
    lane = lax.broadcasted_iota(jnp.int32, (8, 128), 1)
    window = 8 * sub + (lane & 63)
    even_lane = lane < 64
    kappa_lane = (lane >= 44) & (lane < 56)
    kappa_rows = jnp.broadcast_to(kappa_ref[...], (8, 128))
    shifted_field = [pltpu.roll(field_ref[...], 16, 1), pltpu.roll(field_ref[...], 512 - 48, 1)]
    shifted_heat = [pltpu.roll(heat_ref[...], 16, 1), pltpu.roll(heat_ref[...], 512 - 48, 1)]

    def windows(shifted, m):
        part = shifted[m % 2][:, 128 * (m // 2) : 128 * (m // 2) + 128]
        even = take_lanes(jnp.broadcast_to(part[0:1], (8, 128)), window)
        odd = take_lanes(jnp.broadcast_to(part[1:2], (8, 128)), window)
        return jnp.where(even_lane, even, odd)

    for m in range(slabs // 8):
        outbox[8 * m : 8 * m + 8, 0:128] = windows(shifted_field, m)
        index = (2 * (8 * m + sub) - 4 + lane - 44) & 127
        outbox[8 * m : 8 * m + 8, 128:256] = jnp.where(
            kappa_lane, take_lanes(kappa_rows, index), windows(shifted_heat, m)
        )

    expected = (
        jnp.where(ordered, rank, slabs - 1)
        + jnp.where(g > 0, 2, 1)
        + jnp.where(sends_low, slabs, 0)
        + jnp.where(sends_high, slabs, 0)
    )
    for to_g, to_h, inside, upper in near_to.values():
        expected = expected + jnp.where(jnp.logical_not(inside | upper), 1, 0)

    @pl.when(ordered)
    def _():
        pl.semaphore_wait(barrier, expected)

    def remote(source, target, send_sem, recv_sem, device):
        return pltpu.make_async_remote_copy(
            src_ref=source,
            dst_ref=target,
            send_sem=send_sem,
            recv_sem=recv_sem,
            device_id=device,
            device_id_type=MESH,
        )

    def start_if(condition, copy):
        @pl.when(condition)
        def _():
            copy.start()

    def wait_messages(many, sem):
        size = tally.at[pl.ds(0, many)]
        pltpu.make_async_copy(size, size, sem).wait()

    def post(device, target_row, send_sem, recv_sem):
        return remote(
            outbox.at[pl.ds(device[1], 1), :],
            inbox.at[pl.ds(target_row, 1), :],
            send_sem,
            recv_sem,
            device,
        )

    near = {}
    for by in (1, -1, 2, -2):
        to_g, to_h, inside, upper = near_to[by]
        slot = {2: 0, 1: 1, -1: 2, -2: 3}[by]
        pairs = [(field_ref, near_field, slot, 0)]
        if by in (1, -1):
            pairs.append((heat_ref, near_heat, slot - 1, 1))
        if by != -2:
            pairs.append((kappa_ref, near_kappa, slot, 2))
        near[by] = [
            remote(
                source,
                target.at[place_],
                near_send_sems.at[slot, kind],
                near_sems.at[slot, kind],
                (to_g, to_h),
            )
            for source, target, place_, kind in pairs
        ]
        for copy in near[by]:
            start_if(ordered & jnp.logical_not(upper), copy)

    slot_low = jnp.minimum(h, 2) + 2
    slot_high = jnp.maximum(h - (slabs - 2), 0)

    def fan_high():
        def body(to_h, carry):
            post((g_next, to_h), slot_high, box_sems.at[1], row_sems.at[slot_high]).start()
            return carry

        lax.fori_loop(0, slabs, body, 0)

    pl.when(ordered & sends_high)(fan_high)

    for copy in loads[3:]:
        copy.wait()
    weight = 1 << (2 * lax.broadcasted_iota(jnp.int32, (6, 1), 0))
    codes = jnp.sum((table_ref[...] - 1) * weight, axis=0, keepdims=True)
    for row in range(31):
        low_half = codes[:, 256 * row : 256 * row + 128]
        high_half = codes[:, 256 * row + 128 : 256 * row + 256]
        words[8 * row : 8 * row + 8, :] = jnp.broadcast_to(
            low_half | (high_half << 12), (8, 128)
        )
    rest = jnp.concatenate([codes[:, 7936:8000], jnp.zeros((1, 64), jnp.int32)], 1)
    words[248:256, :] = jnp.broadcast_to(rest, (8, 128))

    edge_x = solid_ref.shape[0]

    def weighted_by(code, solid, d):
        return (0.25 * solid) * (((code >> (2 * d)) & 3) + 1).astype(jnp.float32)

    edge_low[...] = weighted_by(lookup(words, label_ref[0:8, :]), solid_ref[0:8, :], 0)
    edge_high[...] = weighted_by(
        lookup(words, label_ref[edge_x - 8 : edge_x, :]), solid_ref[edge_x - 8 : edge_x, :], 1
    )

    lane_c = lax.broadcasted_iota(jnp.int32, (CHUNK, 128), 1)
    depth = lane_c & 15

    def cells(c, carry):
        rows = pl.ds(pl.multiple_of(c * CHUNK, CHUNK), CHUNK)
        labels = label_ref[rows, :]
        code = jnp.concatenate(
            [lookup(words, labels[8 * k : 8 * k + 8]) for k in range(CHUNK // 8)], 0
        )
        quarter = 0.25 * solid_ref[rows, :]

        def weighted(d):
            return quarter * (((code >> (2 * d)) & 3) + 1).astype(jnp.float32)

        ahead_x[rows, :] = weighted(0)
        behind_x[rows, :] = weighted(1)
        up_y = weighted(2)
        down_y = weighted(3)
        up_z = weighted(4)
        down_z = weighted(5)
        gathered[rows, :] = (
            jnp.where(depth == 15, pltpu.roll(up_z, 15, 1), pltpu.roll(up_z, 127, 1))
            + jnp.where(depth == 0, pltpu.roll(down_z, 113, 1), pltpu.roll(down_z, 1, 1))
            + jnp.where(lane_c < 112, pltpu.roll(up_y, 112, 1), 0.0)
            + jnp.where(lane_c >= 16, pltpu.roll(down_y, 16, 1), 0.0)
        )
        mine = (lane_c >> 4) == c
        ahead_y[...] = jnp.where(mine, pltpu.roll(up_y, 16 * c, 1), ahead_y[...])
        behind_y[...] = jnp.where(
            mine, pltpu.roll(down_y, lax.rem(16 * c + 16, 128), 1), behind_y[...]
        )
        return carry

    ahead_y[...] = jnp.zeros(ahead_y.shape, jnp.float32)
    behind_y[...] = jnp.zeros(behind_y.shape, jnp.float32)
    chunks = edge_x // CHUNK
    hops = jnp.abs(lax.rem(h // 2, 4) - 2) + jnp.abs(h // 8 - 4)
    ahead = jnp.where(g == 0, chunks, jnp.where(ordered, 0, jnp.minimum(2 * hops, chunks)))
    lax.fori_loop(0, ahead, cells, 0)

    @pl.when(jnp.logical_not(ordered))
    def _():
        pl.semaphore_wait(barrier, expected)

    to_prev = remote(edge_low, from_ahead_x, edge_send_sems.at[2], edge_recv_sems.at[2], (g_prev, h))
    to_next = remote(edge_high, from_behind_x, edge_send_sems.at[3], edge_recv_sems.at[3], (g_next, h))
    start_if(jnp.logical_not(prev_upper), to_prev)
    to_next.start()

    for by in (1, -1, 2, -2):
        for copy in near[by]:
            start_if(jnp.logical_not(ordered | near_to[by][3]), copy)

    @pl.when(sends_low)
    def _():
        def body(to_h, carry):
            post((g_prev, to_h), slabs + slot_low, box_sems.at[1], row_sems.at[slot_low]).start()
            return carry

        lax.fori_loop(0, slabs, body, 0)

    pl.when(jnp.logical_not(ordered) & sends_high)(fan_high)

    kind = jnp.where(at_low, 3, 2)
    own = pltpu.make_async_copy(
        outbox.at[pl.ds(h, 1), :], inbox.at[pl.ds(h + 2, 1), :], box_sems.at[kind]
    )
    own.start()

    def post_group(r, carry):
        post((g, place(r)), h + 2, box_sems.at[0], box_sems.at[kind]).start()
        return carry

    def answer(r, carry):
        pl.semaphore_signal(
            ready_sem, inc=1, device_id=(g, place(r)), device_id_type=MESH
        )
        return carry

    def post_above(step, carry):
        post((g, place(slabs - 1 - step)), h + 2, box_sems.at[0], box_sems.at[kind]).start()
        return carry

    lax.fori_loop(0, jnp.where(ordered, rank, 0), answer, 0)
    lax.fori_loop(0, jnp.where(ordered, 0, slabs - 1 - rank), post_above, 0)
    lax.fori_loop(0, rank, post_group, 0)

    lax.fori_loop(ahead, chunks, cells, 0)

    total = jnp.zeros((edge_x, 128), jnp.float32)
    cell_row = lax.broadcasted_iota(jnp.int32, (edge_x, 128), 0)
    cell_lane = lax.broadcasted_iota(jnp.int32, (128, 128), 0)
    for part in range(2):
        slots = slot_ref[part : part + 1, :]
        code = lookup(words, jnp.broadcast_to(seed_ref[part : part + 1, :], (8, 128)))
        level = jnp.full((8, 128), 6, jnp.int32)
        for d in range(6):
            level = level + ((code >> (2 * d)) & 3)
        level = level[0:1].astype(jnp.float32)
        at_row = jnp.where(cell_row == (slots >> 7), 1.0, 0.0).astype(jnp.bfloat16)
        at_lane = jnp.where(cell_lane == (slots & 127), level, 0.0).astype(jnp.bfloat16)
        total = total + lax.dot_general(
            at_row, at_lane, (((1,), (1,)), ((), ())), preferred_element_type=jnp.float32
        )
    nucleation[...] = total * (1.0 / 6.0)

    h_next = lax.rem(h + 1, slabs)
    h_prev = lax.rem(h + slabs - 1, slabs)
    down_y_copy = remote(
        ahead_y, from_ahead_y, edge_send_sems.at[0], edge_recv_sems.at[0], (g, h_prev)
    )
    up_y_copy = remote(
        behind_y, from_behind_y, edge_send_sems.at[1], edge_recv_sems.at[1], (g, h_next)
    )

    prev_above = ordered & (rank_of(h_prev) > rank)
    next_above = ordered & (rank_of(h_next) > rank)
    start_if(jnp.logical_not(prev_above), down_y_copy)
    start_if(jnp.logical_not(next_above), up_y_copy)

    gathered[0 : edge_x - 1, :] = gathered[0 : edge_x - 1, :] + ahead_x[1:edge_x, :]
    gathered[1:edge_x, :] = gathered[1:edge_x, :] + behind_x[0 : edge_x - 1, :]

    @pl.when(ordered & (rank < slabs - 1))
    def _():
        pl.semaphore_wait(ready_sem, slabs - 1 - rank)

    lax.fori_loop(0, jnp.where(ordered, slabs - 1 - rank, 0), post_above, 0)
    start_if(prev_above, down_y_copy)
    start_if(next_above, up_y_copy)
    for by in (1, -1, 2, -2):
        to_g, to_h, inside, upper = near_to[by]
        for copy in near[by]:
            start_if(upper & inside, copy)

    wait_messages(3, box_sems.at[3])

    to_prev_rows = [
        remote(
            inbox.at[pl.ds(2 + k, 1), :],
            inbox.at[pl.ds(slabs + 2 + k, 1), :],
            forward_sems.at[k],
            row_sems.at[2 + k],
            (g_prev, h),
        )
        for k in range(3)
    ]
    for copy in to_prev_rows:
        start_if(ordered, copy)
    wait_messages(slabs - 3, box_sems.at[2])

    for by in (1, -1, 2, -2):
        to_g, to_h, inside, upper = near_to[by]

        @pl.when(upper & jnp.logical_not(inside))
        def _(by=by):
            for copy in near[-by]:
                copy.wait_recv()
            for copy in near[by]:
                copy.start()

    @pl.when(prev_upper)
    def _():
        to_next.wait_recv()
        to_prev.start()

    for copy in to_prev_rows:
        start_if(prev_upper, copy)

    for by in (1, -1, 2, -2):

        @pl.when(near_to[-by][2] | jnp.logical_not(near_to[-by][3]))
        def _(by=by):
            for copy in near[by]:
                copy.wait_recv()

    zero = jnp.zeros((8, 128), jnp.float32)
    stacked_field = jnp.stack(
        [
            blocks(near_field[0]),
            blocks(near_field[1]),
            blocks(field_ref[...]),
            blocks(near_field[2]),
            blocks(near_field[3]),
        ],
        0,
    )
    stacked_heat = jnp.stack(
        [zero, blocks(near_heat[0]), blocks(heat_ref[...]), blocks(near_heat[1]), zero], 0
    )

    block_of = sub >> 1

    def expanded(row):
        index = block_of * 32 + (lane >> 3) * 2 + ((lane >> 1) & 1)
        return take_lanes(jnp.broadcast_to(row, (8, 128)), index)

    stacked_kappa = jnp.stack(
        [
            expanded(near_kappa[0]),
            expanded(near_kappa[1]),
            expanded(kappa_ref[...]),
            expanded(near_kappa[2]),
            zero,
        ],
        0,
    )
    moved = heat_step(
        stacked_field, stacked_heat, stacked_kappa, SlabShifts((5, 8, 128))
    )[2]
    for q in range(4):
        new_field_ref[:, 128 * q : 128 * q + 128] = moved[2 * q : 2 * q + 2, :]

    for number in range(5):
        wait_messages(1, row_sems.at[number])
    shifts = BrickShifts((ROWS, 128))
    box_lane = lax.broadcasted_iota(jnp.int32, (ROWS, 128), 1)
    half = box_lane & 63
    brick_heat = inbox[:, 128:256]
    brick_kappa = take_lanes(
        brick_heat, jnp.minimum(44 + (half >> 3) * 2 + ((half >> 1) & 1), 55)
    )
    brick = heat_step(inbox[:, 0:128], brick_heat, brick_kappa, shifts)
    box_row = lax.broadcasted_iota(jnp.int32, (ROWS, 128), 0)
    wanted = (half >= 16) & (half < 28) & (box_row >= 2) & (box_row < slabs + 3)
    brick = pltpu.roll(jnp.where(wanted, brick, 0.0), ROWS - 2, 0)
    pair = jnp.dot(
        brick, matrix_ref[...], precision=HIGHEST, preferred_element_type=jnp.float32
    )
    planes[:, 0:256] = pair
    planes[:, 256:384] = pltpu.roll(pair[:, 0:128], ROWS - 1, 0)

    down_y_copy.wait_recv()
    up_y_copy.wait_recv()

    to_prev.wait_recv()

    @pl.when(jnp.logical_not(prev_upper))
    def _():
        to_next.wait_recv()

    gathered[edge_x - 1 : edge_x, :] = gathered[edge_x - 1 : edge_x, :] + from_ahead_x[0:1, :]
    gathered[0:1, :] = gathered[0:1, :] + from_behind_x[7:8, :]
    side_ahead[...] = from_ahead_y[...]
    side_behind[...] = from_behind_y[...]

    for copies in near.values():
        for copy in copies:
            copy.wait_send()
    for copy in (down_y_copy, up_y_copy, to_prev, to_next):
        copy.wait_send()
    wait_messages(slabs - 1, box_sems.at[0])

    @pl.when(sends_low | sends_high)
    def _():
        wait_messages(slabs, box_sems.at[1])

    @pl.when(prev_upper | ordered)
    def _():
        for copy in to_prev_rows:
            copy.wait_send()


def finish(
    field_ref,
    solid_ref,
    planes,
    gathered,
    nucleation,
    side_ahead,
    side_behind,
    new_field_any,
    new_solid_any,
    result,
    sems,
):
    chunks = solid_ref.shape[0] // CHUNK
    field_out = pltpu.make_async_copy(field_ref, new_field_any, sems.at[chunks])
    field_out.start()
    sub = lax.broadcasted_iota(jnp.int32, (8, 128), 0)
    lane_c = lax.broadcasted_iota(jnp.int32, (CHUNK, 128), 1)
    point = (sub.astype(jnp.float32) + 0.5) * 0.125
    basis = (
        2.0 * (point - 0.5) * (point - 1.0),
        -4.0 * point * (point - 1.0),
        2.0 * point * (point - 0.5),
    )
    stores = []
    for c in range(chunks):
        rows = slice(c * CHUNK, (c + 1) * CHUNK)
        layer = planes[c * (CHUNK // 8) : (c + 1) * (CHUNK // 8), :]
        parts = []
        for k in range(CHUNK // 8):
            parts.append(
                basis[0] * layer[k : k + 1, 0:128]
                + basis[1] * layer[k : k + 1, 128:256]
                + basis[2] * layer[k : k + 1, 256:384]
            )
        under = jnp.maximum(-jnp.concatenate(parts, 0), 0.0)
        side = jnp.where(
            lane_c >= 112,
            pltpu.roll(side_ahead[...], (240 - 16 * c) % 128, 1),
            jnp.where(lane_c < 16, pltpu.roll(side_behind[...], (128 - 16 * c) % 128, 1), 0.0),
        )
        rate = under * (under * (gathered[rows, :] + side) + nucleation[rows, :])
        solid = solid_ref[rows, :]
        result[rows, :] = solid + (1.0 - solid) * (1.0 - jnp.exp(-rate))
        copy = pltpu.make_async_copy(result.at[rows, :], new_solid_any.at[rows, :], sems.at[c])
        copy.start()
        stores.append(copy)
    for copy in stores:
        copy.wait()
    field_out.wait()


def solution(mesh):
    groups, slabs = mesh.shape["grp"], mesh.shape["slab"]
    matrix = interpolation_matrix()

    def body(field, kappa, heat, solid, label, table, slot, seed):
        vmem = pl.BlockSpec(memory_space=pltpu.VMEM)
        anywhere = pl.BlockSpec(memory_space=pl.ANY)
        edge_x = solid.shape[0]
        f32, i32 = jnp.float32, jnp.int32
        cells = (edge_x, 128)
        found = pl.pallas_call(
            functools.partial(exchange, groups, slabs),
            out_shape=(
                jax.ShapeDtypeStruct(field.shape, f32),
                jax.ShapeDtypeStruct(cells, f32),
                jax.ShapeDtypeStruct((ROWS, 384), f32),
                jax.ShapeDtypeStruct(cells, f32),
                jax.ShapeDtypeStruct(cells, f32),
                jax.ShapeDtypeStruct((CHUNK, 128), f32),
                jax.ShapeDtypeStruct((CHUNK, 128), f32),
            ),
            in_specs=[pl.BlockSpec(memory_space=pltpu.HBM)] * 9,
            out_specs=(vmem,) * 7,
            scratch_shapes=[
                pltpu.VMEM(field.shape, f32),
                pltpu.VMEM(kappa.shape, f32),
                pltpu.VMEM(heat.shape, f32),
                pltpu.VMEM(cells, i32),
                pltpu.VMEM(table.shape[::-1], i32),
                pltpu.VMEM((2, 128), i32),
                pltpu.VMEM((2, 128), i32),
                pltpu.VMEM(matrix.shape, f32),
                pltpu.VMEM((slabs, 256), f32),
                pltpu.VMEM((ROWS, 256), f32),
                pltpu.VMEM((4, 2, 512), f32),
                pltpu.VMEM((2, 2, 512), f32),
                pltpu.VMEM((3, 1, 128), f32),
                pltpu.VMEM((256, 128), i32),
                pltpu.VMEM(cells, f32),
                pltpu.VMEM(cells, f32),
                pltpu.VMEM((CHUNK, 128), f32),
                pltpu.VMEM((CHUNK, 128), f32),
                pltpu.VMEM((8, 128), f32),
                pltpu.VMEM((8, 128), f32),
                pltpu.VMEM((CHUNK, 128), f32),
                pltpu.VMEM((CHUNK, 128), f32),
                pltpu.VMEM((slabs, 2, 128), f32),
                pltpu.VMEM((8, 128), f32),
                pltpu.VMEM((8, 128), f32),
                pltpu.SemaphoreType.DMA((9,)),
                pltpu.SemaphoreType.DMA((4,)),
                pltpu.SemaphoreType.DMA((5,)),
                pltpu.SemaphoreType.DMA((3,)),
                pltpu.SemaphoreType.REGULAR,
                pltpu.SemaphoreType.DMA((4, 3)),
                pltpu.SemaphoreType.DMA((4, 3)),
                pltpu.SemaphoreType.DMA((4,)),
                pltpu.SemaphoreType.DMA((4,)),
            ],
            compiler_params=pltpu.CompilerParams(
                collective_id=0, has_side_effects=True, vmem_limit_bytes=16 << 20
            ),
        )(
            *(
                pltpu.with_memory_space_constraint(value, pltpu.HBM)
                for value in (
                    field,
                    kappa,
                    heat,
                    solid,
                    label,
                    table.T,
                    slot.reshape(2, 128),
                    seed.reshape(2, 128),
                    jnp.asarray(matrix),
                )
            )
        )
        return pl.pallas_call(
            finish,
            out_shape=(
                jax.ShapeDtypeStruct(field.shape, f32),
                jax.ShapeDtypeStruct(solid.shape, f32),
            ),
            in_specs=[vmem] * 7,
            out_specs=(anywhere, anywhere),
            scratch_shapes=[
                pltpu.VMEM(cells, f32),
                pltpu.SemaphoreType.DMA((edge_x // CHUNK + 1,)),
            ],
            compiler_params=pltpu.CompilerParams(vmem_limit_bytes=16 << 20),
        )(*found)

    in_specs = (
        P(("grp", "slab"), None),
        P(("grp", "slab"), None),
        P(("grp", "slab"), None),
        P("grp", "slab"),
        P("grp", "slab"),
        P(),
        P(("grp", "slab")),
        P(("grp", "slab")),
    )
    out_specs = (P(("grp", "slab"), None), P("grp", "slab"))
    return jax.shard_map(body, mesh=mesh, in_specs=in_specs, out_specs=out_specs, check_vma=False)
```

```python
import functools

import jax
import jax.numpy as jnp
import numpy as np
from jax import lax
from jax.experimental import pallas as pl
from jax.experimental.pallas import tpu as pltpu
from jax.sharding import PartitionSpec as P

MESH = pl.DeviceIdType.MESH
HIGHEST = lax.Precision.HIGHEST
STEP = 0.004
CHUNK = 64
ROWS = 72


def interpolation_matrix():
    points = (np.arange(8) + 0.5) / 8
    basis = np.stack(
        [
            2.0 * (points - 0.5) * (points - 1.0),
            -4.0 * points * (points - 1.0),
            2.0 * points * (points - 0.5),
        ],
        1,
    )
    along_z = np.zeros((4, 16))
    for c in range(2):
        for p in range(8):
            for k in range(3):
                along_z[(2 * c + k) % 4, 8 * c + p] += basis[p, k]
    plane = np.einsum("nj,zc->jznc", basis, along_z).reshape(12, 128)
    matrix = np.zeros((128, 256), np.float32)
    matrix[16:28, :128] = plane
    matrix[80:92, 128:] = plane
    return matrix


def take_lanes(values, index):
    return jnp.take_along_axis(values, index, axis=1, mode="promise_in_bounds")


def stiffness_action(kappa, shifts):
    odd_x, odd_y, odd_z = shifts.odd

    def spread(values, axis):
        before = shifts.moved(values, axis, -1)
        return jnp.where(
            shifts.odd[axis], (2.0 / 3.0) * values, (1.0 / 6.0) * (values + before)
        )

    def spread_x(values):
        return jnp.where(
            odd_x,
            (2.0 / 3.0) * values,
            (1.0 / 6.0) * (values + shifts.slab(values, -1)),
        )

    over_x = spread_x(kappa)
    fields = (
        spread(spread(kappa, 1), 2) * (1.0 / 3.0),
        spread(over_x, 2) * (1.0 / 3.0),
        spread(over_x, 1) * (1.0 / 3.0),
    )
    centre = None
    pairs = []
    for axis in range(3):
        here = fields[axis]
        if axis == 0:
            before = shifts.slab(here, -1)
        else:
            before = shifts.moved(here, axis, -1)
        part = jnp.where(shifts.odd[axis], 16.0 * here, 7.0 * (here + before))
        centre = part if centre is None else centre + part
        pairs.append((here, jnp.where(shifts.odd[axis], here, before)))

    def act(values):
        total = centre * values
        for axis in range(3):
            ahead, behind = pairs[axis]
            one, two, back, back_two = shifts.neighbours(values, axis)
            odd = shifts.odd[axis]
            total = total + ahead * (jnp.where(odd, 0.0, two) - 8.0 * one)
            total = total + behind * (jnp.where(odd, 0.0, back_two) - 8.0 * back)
        return total

    return act


class Shifts:
    lane_axis = 1

    def lane_roll(self, values, by):
        return pltpu.roll(values, by % 128, self.lane_axis)

    def z_moved(self, values, by):
        z = self.z
        if by == 1:
            return jnp.where(z == 3, self.lane_roll(values, 3), self.lane_roll(values, -1))
        if by == -1:
            return jnp.where(z == 0, self.lane_roll(values, -3), self.lane_roll(values, 1))
        return jnp.where(z >= 2, self.lane_roll(values, 2), self.lane_roll(values, -2))

    def moved(self, values, axis, by):
        if axis == 1:
            return self.y_moved(values, by)
        return self.z_moved(values, by)

    def neighbours(self, values, axis):
        if axis == 0:
            other = self.other(values)
            ahead = jnp.where(self.odd[0], self.slab(other, 1), other)
            behind = jnp.where(self.odd[0], other, self.slab(other, -1))
            return ahead, self.slab(values, 1), behind, self.slab(values, -1)
        if axis == 1:
            return tuple(self.y_moved(values, by) for by in (1, 2, -1, -2))
        two = self.z_moved(values, 2)
        return self.z_moved(values, 1), two, self.z_moved(values, -1), two


class BrickShifts(Shifts):
    def __init__(self, shape):
        lane = lax.broadcasted_iota(jnp.int32, shape, 1)
        self.rows = shape[0]
        self.z = lane & 3
        self.odd = (lane >= 64, (lane & 4) != 0, (lane & 1) != 0)

    def y_moved(self, values, by):
        return self.lane_roll(values, -4 * by)

    def slab(self, values, by):
        return pltpu.roll(values, (-by) % self.rows, 0)

    def other(self, values):
        return self.lane_roll(values, 64)


class SlabShifts(Shifts):
    lane_axis = 2

    def __init__(self, shape):
        self.lane = lax.broadcasted_iota(jnp.int32, shape, 2)
        self.plane = lax.broadcasted_iota(jnp.int32, shape, 1) & 1
        self.z = self.lane & 3
        self.odd = (self.plane != 0, (self.lane & 4) != 0, (self.lane & 1) != 0)

    def y_moved(self, values, by):
        rolled = self.lane_roll(values, -4 * by)
        if by > 0:
            return jnp.where(
                self.lane < 128 - 4 * by, rolled, pltpu.roll(rolled, 6, 1)
            )
        return jnp.where(self.lane >= -4 * by, rolled, pltpu.roll(rolled, 2, 1))

    def slab(self, values, by):
        if by == 1:
            return jnp.concatenate([values[1:], values[:1]], 0)
        return jnp.concatenate([values[-1:], values[:-1]], 0)

    def other(self, values):
        return jnp.where(self.plane == 0, pltpu.roll(values, 7, 1), pltpu.roll(values, 1, 1))


def inverse_mass(shifts):
    odd_x, odd_y, odd_z = shifts.odd
    return (
        jnp.where(odd_x, 1.5, 3.0) * jnp.where(odd_y, 1.5, 3.0) * jnp.where(odd_z, 1.5, 3.0)
    )


def heat_step(field, heat, kappa, shifts):
    act = stiffness_action(kappa, shifts)
    inverse = inverse_mass(shifts)
    rate_one = (heat - act(field)) * inverse
    middle = field + STEP * rate_one
    rate_two = (heat - act(middle)) * inverse
    return field + (0.5 * STEP) * (rate_one + rate_two)


def blocks(values):
    return jnp.concatenate([values[:, 128 * q : 128 * q + 128] for q in range(4)], 0)


def lookup(table_ref, labels):
    low = labels & 127
    bits = [(labels & (256 << level)) != 0 for level in range(5)]

    def choose(first, level):
        if level < 0:
            return take_lanes(table_ref[8 * first : 8 * first + 8, :], low)
        return jnp.where(
            bits[level], choose(first + (1 << level), level - 1), choose(first, level - 1)
        )

    found = choose(0, 4)
    return jnp.where((labels & 128) != 0, found >> 12, found & 4095)


def exchange(
    groups,
    slabs,
    field_any,
    kappa_any,
    heat_any,
    solid_any,
    label_any,
    table_any,
    slot_any,
    seed_any,
    matrix_any,
    new_field_ref,
    solid_ref,
    planes,
    gathered,
    nucleation,
    side_ahead,
    side_behind,
    field_ref,
    kappa_ref,
    heat_ref,
    label_ref,
    table_ref,
    slot_ref,
    seed_ref,
    matrix_ref,
    outbox,
    inbox,
    near_field,
    near_heat,
    near_kappa,
    words,
    ahead_x,
    behind_x,
    ahead_y,
    behind_y,
    from_ahead_x,
    from_behind_x,
    from_ahead_y,
    from_behind_y,
    tally,
    edge_low,
    edge_high,
    load_sems,
    box_sems,
    row_sems,
    forward_sems,
    ready_sem,
    near_sems,
    near_send_sems,
    edge_recv_sems,
    edge_send_sems,
):
    loads = []
    for number, (source, target) in enumerate(
        (
            (field_any, field_ref),
            (heat_any, heat_ref),
            (kappa_any, kappa_ref),
            (table_any, table_ref),
            (label_any, label_ref),
            (solid_any, solid_ref),
            (slot_any, slot_ref),
            (seed_any, seed_ref),
            (matrix_any, matrix_ref),
        )
    ):
        copy = pltpu.make_async_copy(source, target, load_sems.at[number])
        copy.start()
        loads.append(copy)
    g = lax.axis_index("grp")
    h = lax.axis_index("slab")
    g_next = lax.rem(g + 1, groups)
    g_prev = lax.rem(g + groups - 1, groups)

    ordered = g == groups - 1

    rows_y = slabs // 8
    early = 22

    def place(rank):
        at = jnp.where(rank < 2, rank + early, jnp.where(rank < early + 2, rank - 2, rank))
        fold = at >> 3
        row = jnp.where((fold & 1) == 1, (fold + 1) >> 1, 0 - (fold >> 1)) & (rows_y - 1)
        return 8 * row + (at & 7)

    def rank_of(other):
        row = other >> 3
        fold = jnp.where(
            row == 0, 0, jnp.where(row <= rows_y // 2, 2 * row - 1, 2 * (rows_y - row))
        )
        at = 8 * fold + (other & 7)
        return jnp.where(
            other >= slabs - 2, other - (slabs - 2), jnp.where(at < early, at + 2, at)
        )

    rank = rank_of(h)
    prev_upper = g == 0
    at_low, at_high = h <= 2, h >= slabs - 2
    sends_low = at_low & (g > 0) & jnp.logical_not(ordered)
    sends_high = at_high

    barrier = pltpu.get_barrier_semaphore()

    def greet(to_g, to_h):
        pl.semaphore_signal(barrier, inc=1, device_id=(to_g, to_h), device_id_type=MESH)

    greet(g_prev, h)
    for last in range(2):
        greet(g_prev, jnp.int32(slabs - 1 - last))

    @pl.when(jnp.logical_not(ordered))
    def _():
        greet(g_next, h)

    @pl.when(g < groups - 2)
    def _():
        for first in range(3):
            greet(g_next, jnp.int32(first))

    here = g * slabs + h
    count = groups * slabs
    near_to = {}
    for by in (1, -1, 2, -2):
        there = lax.rem(here + by + count, count)
        to_g, to_h = there // slabs, lax.rem(there, slabs)
        inside = to_g == g
        upper = jnp.where(
            inside, ordered & (rank_of(to_h) > rank), prev_upper if by < 0 else False
        )
        silent = ordered if by > 0 else False

        @pl.when(jnp.logical_not(inside | silent))
        def _(to_g=to_g, to_h=to_h):
            greet(to_g, to_h)

        near_to[by] = (to_g, to_h, inside, upper)

    def greet_rank(r, carry):
        greet(g, place(r))
        return carry

    lax.fori_loop(0, jnp.where(ordered, 0, rank), greet_rank, 0)
    lax.fori_loop(rank + 1, slabs, greet_rank, 0)

    for copy in loads[:3]:
        copy.wait()
    sub = lax.broadcasted_iota(jnp.int32, (8, 128), 0)
    lane = lax.broadcasted_iota(jnp.int32, (8, 128), 1)
    window = 8 * sub + (lane & 63)
    even_lane = lane < 64
    kappa_lane = (lane >= 44) & (lane < 56)
    kappa_rows = jnp.broadcast_to(kappa_ref[...], (8, 128))
    shifted_field = [pltpu.roll(field_ref[...], 16, 1), pltpu.roll(field_ref[...], 512 - 48, 1)]
    shifted_heat = [pltpu.roll(heat_ref[...], 16, 1), pltpu.roll(heat_ref[...], 512 - 48, 1)]

    def windows(shifted, m):
        part = shifted[m % 2][:, 128 * (m // 2) : 128 * (m // 2) + 128]
        even = take_lanes(jnp.broadcast_to(part[0:1], (8, 128)), window)
        odd = take_lanes(jnp.broadcast_to(part[1:2], (8, 128)), window)
        return jnp.where(even_lane, even, odd)

    for m in range(slabs // 8):
        outbox[8 * m : 8 * m + 8, 0:128] = windows(shifted_field, m)
        index = (2 * (8 * m + sub) - 4 + lane - 44) & 127
        outbox[8 * m : 8 * m + 8, 128:256] = jnp.where(
            kappa_lane, take_lanes(kappa_rows, index), windows(shifted_heat, m)
        )

    expected = (
        jnp.where(ordered, rank, slabs - 1)
        + jnp.where(g > 0, 2, 1)
        + jnp.where(sends_low, slabs, 0)
        + jnp.where(sends_high, slabs, 0)
    )
    for to_g, to_h, inside, upper in near_to.values():
        expected = expected + jnp.where(jnp.logical_not(inside | upper), 1, 0)

    first = ordered & sends_high

    @pl.when(first)
    def _():
        pl.semaphore_wait(barrier, expected)

    def remote(source, target, send_sem, recv_sem, device):
        return pltpu.make_async_remote_copy(
            src_ref=source,
            dst_ref=target,
            send_sem=send_sem,
            recv_sem=recv_sem,
            device_id=device,
            device_id_type=MESH,
        )

    def start_if(condition, copy):
        @pl.when(condition)
        def _():
            copy.start()

    def wait_messages(many, sem):
        size = tally.at[pl.ds(0, many)]
        pltpu.make_async_copy(size, size, sem).wait()

    def post(device, target_row, send_sem, recv_sem):
        return remote(
            outbox.at[pl.ds(device[1], 1), :],
            inbox.at[pl.ds(target_row, 1), :],
            send_sem,
            recv_sem,
            device,
        )

    near = {}
    for by in (1, -1, 2, -2):
        to_g, to_h, inside, upper = near_to[by]
        slot = {2: 0, 1: 1, -1: 2, -2: 3}[by]
        pairs = [(field_ref, near_field, slot, 0)]
        if by in (1, -1):
            pairs.append((heat_ref, near_heat, slot - 1, 1))
        if by != -2:
            pairs.append((kappa_ref, near_kappa, slot, 2))
        near[by] = [
            remote(
                source,
                target.at[place_],
                near_send_sems.at[slot, kind],
                near_sems.at[slot, kind],
                (to_g, to_h),
            )
            for source, target, place_, kind in pairs
        ]
        for copy in near[by]:
            start_if(first & jnp.logical_not(upper), copy)

    slot_low = jnp.minimum(h, 2) + 2
    slot_high = jnp.maximum(h - (slabs - 2), 0)

    def fan_high():
        def body(to_h, carry):
            post((g_next, to_h), slot_high, box_sems.at[1], row_sems.at[slot_high]).start()
            return carry

        lax.fori_loop(0, slabs, body, 0)

    pl.when(first)(fan_high)

    for copy in loads[3:]:
        copy.wait()
    weight = 1 << (2 * lax.broadcasted_iota(jnp.int32, (6, 1), 0))
    codes = jnp.sum((table_ref[...] - 1) * weight, axis=0, keepdims=True)
    for row in range(31):
        low_half = codes[:, 256 * row : 256 * row + 128]
        high_half = codes[:, 256 * row + 128 : 256 * row + 256]
        words[8 * row : 8 * row + 8, :] = jnp.broadcast_to(
            low_half | (high_half << 12), (8, 128)
        )
    rest = jnp.concatenate([codes[:, 7936:8000], jnp.zeros((1, 64), jnp.int32)], 1)
    words[248:256, :] = jnp.broadcast_to(rest, (8, 128))

    edge_x = solid_ref.shape[0]

    def weighted_by(code, solid, d):
        return (0.25 * solid) * (((code >> (2 * d)) & 3) + 1).astype(jnp.float32)

    edge_low[...] = weighted_by(lookup(words, label_ref[0:8, :]), solid_ref[0:8, :], 0)
    edge_high[...] = weighted_by(
        lookup(words, label_ref[edge_x - 8 : edge_x, :]), solid_ref[edge_x - 8 : edge_x, :], 1
    )

    lane_c = lax.broadcasted_iota(jnp.int32, (CHUNK, 128), 1)
    depth = lane_c & 15

    def cells(c, carry):
        rows = pl.ds(pl.multiple_of(c * CHUNK, CHUNK), CHUNK)
        labels = label_ref[rows, :]
        code = jnp.concatenate(
            [lookup(words, labels[8 * k : 8 * k + 8]) for k in range(CHUNK // 8)], 0
        )
        quarter = 0.25 * solid_ref[rows, :]

        def weighted(d):
            return quarter * (((code >> (2 * d)) & 3) + 1).astype(jnp.float32)

        ahead_x[rows, :] = weighted(0)
        behind_x[rows, :] = weighted(1)
        up_y = weighted(2)
        down_y = weighted(3)
        up_z = weighted(4)
        down_z = weighted(5)
        gathered[rows, :] = (
            jnp.where(depth == 15, pltpu.roll(up_z, 15, 1), pltpu.roll(up_z, 127, 1))
            + jnp.where(depth == 0, pltpu.roll(down_z, 113, 1), pltpu.roll(down_z, 1, 1))
            + jnp.where(lane_c < 112, pltpu.roll(up_y, 112, 1), 0.0)
            + jnp.where(lane_c >= 16, pltpu.roll(down_y, 16, 1), 0.0)
        )
        mine = (lane_c >> 4) == c
        ahead_y[...] = jnp.where(mine, pltpu.roll(up_y, 16 * c, 1), ahead_y[...])
        behind_y[...] = jnp.where(
            mine, pltpu.roll(down_y, lax.rem(16 * c + 16, 128), 1), behind_y[...]
        )
        return carry

    ahead_y[...] = jnp.zeros(ahead_y.shape, jnp.float32)
    behind_y[...] = jnp.zeros(behind_y.shape, jnp.float32)
    chunks = edge_x // CHUNK
    x, y = (h >> 1) & 3, h >> 3
    hops = jnp.abs(x - 2) + jnp.abs(y - 4)
    last_ahead = jnp.maximum(chunks - 2 * x - jnp.where(y >= 4, 4, 0), 0)
    ahead = jnp.where(
        g == 0,
        chunks,
        jnp.where(
            first, 0, jnp.where(ordered, last_ahead, jnp.minimum(2 * hops, chunks))
        ),
    )
    lax.fori_loop(0, ahead, cells, 0)

    @pl.when(jnp.logical_not(first))
    def _():
        pl.semaphore_wait(barrier, expected)

    to_prev = remote(edge_low, from_ahead_x, edge_send_sems.at[2], edge_recv_sems.at[2], (g_prev, h))
    to_next = remote(edge_high, from_behind_x, edge_send_sems.at[3], edge_recv_sems.at[3], (g_next, h))
    start_if(jnp.logical_not(prev_upper), to_prev)
    to_next.start()

    for by in (1, -1, 2, -2):
        for copy in near[by]:
            start_if(jnp.logical_not(first | near_to[by][3]), copy)

    @pl.when(sends_low)
    def _():
        def body(to_h, carry):
            post((g_prev, to_h), slabs + slot_low, box_sems.at[1], row_sems.at[slot_low]).start()
            return carry

        lax.fori_loop(0, slabs, body, 0)

    pl.when(jnp.logical_not(ordered) & sends_high)(fan_high)

    kind = jnp.where(at_low, 3, 2)
    own = pltpu.make_async_copy(
        outbox.at[pl.ds(h, 1), :], inbox.at[pl.ds(h + 2, 1), :], box_sems.at[kind]
    )
    own.start()

    def post_group(r, carry):
        post((g, place(r)), h + 2, box_sems.at[0], box_sems.at[kind]).start()
        return carry

    def answer(r, carry):
        pl.semaphore_signal(
            ready_sem, inc=1, device_id=(g, place(r)), device_id_type=MESH
        )
        return carry

    def post_above(step, carry):
        post((g, place(slabs - 1 - step)), h + 2, box_sems.at[0], box_sems.at[kind]).start()
        return carry

    lax.fori_loop(0, jnp.where(ordered, rank, 0), answer, 0)
    lax.fori_loop(0, jnp.where(ordered, 0, slabs - 1 - rank), post_above, 0)
    lax.fori_loop(0, rank, post_group, 0)

    lax.fori_loop(ahead, chunks, cells, 0)

    total = jnp.zeros((edge_x, 128), jnp.float32)
    cell_row = lax.broadcasted_iota(jnp.int32, (edge_x, 128), 0)
    cell_lane = lax.broadcasted_iota(jnp.int32, (128, 128), 0)
    for part in range(2):
        slots = slot_ref[part : part + 1, :]
        code = lookup(words, jnp.broadcast_to(seed_ref[part : part + 1, :], (8, 128)))
        level = jnp.full((8, 128), 6, jnp.int32)
        for d in range(6):
            level = level + ((code >> (2 * d)) & 3)
        level = level[0:1].astype(jnp.float32)
        at_row = jnp.where(cell_row == (slots >> 7), 1.0, 0.0).astype(jnp.bfloat16)
        at_lane = jnp.where(cell_lane == (slots & 127), level, 0.0).astype(jnp.bfloat16)
        total = total + lax.dot_general(
            at_row, at_lane, (((1,), (1,)), ((), ())), preferred_element_type=jnp.float32
        )
    nucleation[...] = total * (1.0 / 6.0)

    h_next = lax.rem(h + 1, slabs)
    h_prev = lax.rem(h + slabs - 1, slabs)
    down_y_copy = remote(
        ahead_y, from_ahead_y, edge_send_sems.at[0], edge_recv_sems.at[0], (g, h_prev)
    )
    up_y_copy = remote(
        behind_y, from_behind_y, edge_send_sems.at[1], edge_recv_sems.at[1], (g, h_next)
    )

    prev_above = ordered & (rank_of(h_prev) > rank)
    next_above = ordered & (rank_of(h_next) > rank)
    start_if(jnp.logical_not(prev_above), down_y_copy)
    start_if(jnp.logical_not(next_above), up_y_copy)

    gathered[0 : edge_x - 1, :] = gathered[0 : edge_x - 1, :] + ahead_x[1:edge_x, :]
    gathered[1:edge_x, :] = gathered[1:edge_x, :] + behind_x[0 : edge_x - 1, :]

    @pl.when(ordered & (rank < slabs - 1))
    def _():
        pl.semaphore_wait(ready_sem, slabs - 1 - rank)

    lax.fori_loop(0, jnp.where(ordered, slabs - 1 - rank, 0), post_above, 0)
    start_if(prev_above, down_y_copy)
    start_if(next_above, up_y_copy)
    for by in (1, -1, 2, -2):
        to_g, to_h, inside, upper = near_to[by]
        for copy in near[by]:
            start_if(upper & inside, copy)

    wait_messages(3, box_sems.at[3])

    to_prev_rows = [
        remote(
            inbox.at[pl.ds(2 + k, 1), :],
            inbox.at[pl.ds(slabs + 2 + k, 1), :],
            forward_sems.at[k],
            row_sems.at[2 + k],
            (g_prev, h),
        )
        for k in range(3)
    ]
    for copy in to_prev_rows:
        start_if(ordered, copy)
    wait_messages(slabs - 3, box_sems.at[2])

    for by in (1, -1, 2, -2):
        to_g, to_h, inside, upper = near_to[by]

        @pl.when(upper & jnp.logical_not(inside))
        def _(by=by):
            for copy in near[-by]:
                copy.wait_recv()
            for copy in near[by]:
                copy.start()

    for by in (1, -1, 2, -2):

        @pl.when(near_to[-by][2] | jnp.logical_not(near_to[-by][3]))
        def _(by=by):
            for copy in near[by]:
                copy.wait_recv()

    zero = jnp.zeros((8, 128), jnp.float32)
    stacked_field = jnp.stack(
        [
            blocks(near_field[0]),
            blocks(near_field[1]),
            blocks(field_ref[...]),
            blocks(near_field[2]),
            blocks(near_field[3]),
        ],
        0,
    )
    stacked_heat = jnp.stack(
        [zero, blocks(near_heat[0]), blocks(heat_ref[...]), blocks(near_heat[1]), zero], 0
    )

    block_of = sub >> 1

    def expanded(row):
        index = block_of * 32 + (lane >> 3) * 2 + ((lane >> 1) & 1)
        return take_lanes(jnp.broadcast_to(row, (8, 128)), index)

    stacked_kappa = jnp.stack(
        [
            expanded(near_kappa[0]),
            expanded(near_kappa[1]),
            expanded(kappa_ref[...]),
            expanded(near_kappa[2]),
            zero,
        ],
        0,
    )
    moved = heat_step(
        stacked_field, stacked_heat, stacked_kappa, SlabShifts((5, 8, 128))
    )[2]
    for q in range(4):
        new_field_ref[:, 128 * q : 128 * q + 128] = moved[2 * q : 2 * q + 2, :]

    @pl.when(prev_upper)
    def _():
        to_next.wait_recv()
        to_prev.start()

    for copy in to_prev_rows:
        start_if(prev_upper, copy)

    for number in range(5):
        wait_messages(1, row_sems.at[number])
    shifts = BrickShifts((ROWS, 128))
    box_lane = lax.broadcasted_iota(jnp.int32, (ROWS, 128), 1)
    half = box_lane & 63
    brick_heat = inbox[:, 128:256]
    brick_kappa = take_lanes(
        brick_heat, jnp.minimum(44 + (half >> 3) * 2 + ((half >> 1) & 1), 55)
    )
    brick = heat_step(inbox[:, 0:128], brick_heat, brick_kappa, shifts)
    box_row = lax.broadcasted_iota(jnp.int32, (ROWS, 128), 0)
    wanted = (half >= 16) & (half < 28) & (box_row >= 2) & (box_row < slabs + 3)
    brick = pltpu.roll(jnp.where(wanted, brick, 0.0), ROWS - 2, 0)
    pair = jnp.dot(
        brick, matrix_ref[...], precision=HIGHEST, preferred_element_type=jnp.float32
    )
    planes[:, 0:256] = pair
    planes[:, 256:384] = pltpu.roll(pair[:, 0:128], ROWS - 1, 0)

    down_y_copy.wait_recv()
    up_y_copy.wait_recv()

    to_prev.wait_recv()

    @pl.when(jnp.logical_not(prev_upper))
    def _():
        to_next.wait_recv()

    gathered[edge_x - 1 : edge_x, :] = gathered[edge_x - 1 : edge_x, :] + from_ahead_x[0:1, :]
    gathered[0:1, :] = gathered[0:1, :] + from_behind_x[7:8, :]
    side_ahead[...] = from_ahead_y[...]
    side_behind[...] = from_behind_y[...]

    for copies in near.values():
        for copy in copies:
            copy.wait_send()
    for copy in (down_y_copy, up_y_copy, to_prev, to_next):
        copy.wait_send()
    wait_messages(slabs - 1, box_sems.at[0])

    @pl.when(sends_low | sends_high)
    def _():
        wait_messages(slabs, box_sems.at[1])

    @pl.when(prev_upper | ordered)
    def _():
        for copy in to_prev_rows:
            copy.wait_send()


def finish(
    field_ref,
    solid_ref,
    planes,
    gathered,
    nucleation,
    side_ahead,
    side_behind,
    new_field_any,
    new_solid_any,
    result,
    sems,
):
    chunks = solid_ref.shape[0] // CHUNK
    field_out = pltpu.make_async_copy(field_ref, new_field_any, sems.at[chunks])
    field_out.start()
    sub = lax.broadcasted_iota(jnp.int32, (8, 128), 0)
    lane_c = lax.broadcasted_iota(jnp.int32, (CHUNK, 128), 1)
    point = (sub.astype(jnp.float32) + 0.5) * 0.125
    basis = (
        2.0 * (point - 0.5) * (point - 1.0),
        -4.0 * point * (point - 1.0),
        2.0 * point * (point - 0.5),
    )
    stores = []
    for c in range(chunks):
        rows = slice(c * CHUNK, (c + 1) * CHUNK)
        layer = planes[c * (CHUNK // 8) : (c + 1) * (CHUNK // 8), :]
        parts = []
        for k in range(CHUNK // 8):
            parts.append(
                basis[0] * layer[k : k + 1, 0:128]
                + basis[1] * layer[k : k + 1, 128:256]
                + basis[2] * layer[k : k + 1, 256:384]
            )
        under = jnp.maximum(-jnp.concatenate(parts, 0), 0.0)
        side = jnp.where(
            lane_c >= 112,
            pltpu.roll(side_ahead[...], (240 - 16 * c) % 128, 1),
            jnp.where(lane_c < 16, pltpu.roll(side_behind[...], (128 - 16 * c) % 128, 1), 0.0),
        )
        rate = under * (under * (gathered[rows, :] + side) + nucleation[rows, :])
        solid = solid_ref[rows, :]
        result[rows, :] = solid + (1.0 - solid) * (1.0 - jnp.exp(-rate))
        copy = pltpu.make_async_copy(result.at[rows, :], new_solid_any.at[rows, :], sems.at[c])
        copy.start()
        stores.append(copy)
    for copy in stores:
        copy.wait()
    field_out.wait()


def solution(mesh):
    groups, slabs = mesh.shape["grp"], mesh.shape["slab"]
    matrix = interpolation_matrix()

    def body(field, kappa, heat, solid, label, table, slot, seed):
        vmem = pl.BlockSpec(memory_space=pltpu.VMEM)
        anywhere = pl.BlockSpec(memory_space=pl.ANY)
        edge_x = solid.shape[0]
        f32, i32 = jnp.float32, jnp.int32
        cells = (edge_x, 128)
        found = pl.pallas_call(
            functools.partial(exchange, groups, slabs),
            out_shape=(
                jax.ShapeDtypeStruct(field.shape, f32),
                jax.ShapeDtypeStruct(cells, f32),
                jax.ShapeDtypeStruct((ROWS, 384), f32),
                jax.ShapeDtypeStruct(cells, f32),
                jax.ShapeDtypeStruct(cells, f32),
                jax.ShapeDtypeStruct((CHUNK, 128), f32),
                jax.ShapeDtypeStruct((CHUNK, 128), f32),
            ),
            in_specs=[pl.BlockSpec(memory_space=pltpu.HBM)] * 9,
            out_specs=(vmem,) * 7,
            scratch_shapes=[
                pltpu.VMEM(field.shape, f32),
                pltpu.VMEM(kappa.shape, f32),
                pltpu.VMEM(heat.shape, f32),
                pltpu.VMEM(cells, i32),
                pltpu.VMEM(table.shape[::-1], i32),
                pltpu.VMEM((2, 128), i32),
                pltpu.VMEM((2, 128), i32),
                pltpu.VMEM(matrix.shape, f32),
                pltpu.VMEM((slabs, 256), f32),
                pltpu.VMEM((ROWS, 256), f32),
                pltpu.VMEM((4, 2, 512), f32),
                pltpu.VMEM((2, 2, 512), f32),
                pltpu.VMEM((3, 1, 128), f32),
                pltpu.VMEM((256, 128), i32),
                pltpu.VMEM(cells, f32),
                pltpu.VMEM(cells, f32),
                pltpu.VMEM((CHUNK, 128), f32),
                pltpu.VMEM((CHUNK, 128), f32),
                pltpu.VMEM((8, 128), f32),
                pltpu.VMEM((8, 128), f32),
                pltpu.VMEM((CHUNK, 128), f32),
                pltpu.VMEM((CHUNK, 128), f32),
                pltpu.VMEM((slabs, 2, 128), f32),
                pltpu.VMEM((8, 128), f32),
                pltpu.VMEM((8, 128), f32),
                pltpu.SemaphoreType.DMA((9,)),
                pltpu.SemaphoreType.DMA((4,)),
                pltpu.SemaphoreType.DMA((5,)),
                pltpu.SemaphoreType.DMA((3,)),
                pltpu.SemaphoreType.REGULAR,
                pltpu.SemaphoreType.DMA((4, 3)),
                pltpu.SemaphoreType.DMA((4, 3)),
                pltpu.SemaphoreType.DMA((4,)),
                pltpu.SemaphoreType.DMA((4,)),
            ],
            compiler_params=pltpu.CompilerParams(
                collective_id=0, has_side_effects=True, vmem_limit_bytes=16 << 20
            ),
        )(
            *(
                pltpu.with_memory_space_constraint(value, pltpu.HBM)
                for value in (
                    field,
                    kappa,
                    heat,
                    solid,
                    label,
                    table.T,
                    slot.reshape(2, 128),
                    seed.reshape(2, 128),
                    jnp.asarray(matrix),
                )
            )
        )
        return pl.pallas_call(
            finish,
            out_shape=(
                jax.ShapeDtypeStruct(field.shape, f32),
                jax.ShapeDtypeStruct(solid.shape, f32),
            ),
            in_specs=[vmem] * 7,
            out_specs=(anywhere, anywhere),
            scratch_shapes=[
                pltpu.VMEM(cells, f32),
                pltpu.SemaphoreType.DMA((edge_x // CHUNK + 1,)),
            ],
            compiler_params=pltpu.CompilerParams(vmem_limit_bytes=16 << 20),
        )(*found)

    in_specs = (
        P(("grp", "slab"), None),
        P(("grp", "slab"), None),
        P(("grp", "slab"), None),
        P("grp", "slab"),
        P("grp", "slab"),
        P(),
        P(("grp", "slab")),
        P(("grp", "slab")),
    )
    out_specs = (P(("grp", "slab"), None), P("grp", "slab"))
    return jax.shard_map(body, mesh=mesh, in_specs=in_specs, out_specs=out_specs, check_vma=False)
```

```python
import functools

import jax
import jax.numpy as jnp
import numpy as np
from jax import lax
from jax.experimental import pallas as pl
from jax.experimental.pallas import tpu as pltpu
from jax.sharding import PartitionSpec as P

MESH = pl.DeviceIdType.MESH
HIGHEST = lax.Precision.HIGHEST
STEP = 0.004
CHUNK = 64
ROWS = 72


def interpolation_matrix():
    points = (np.arange(8) + 0.5) / 8
    basis = np.stack(
        [
            2.0 * (points - 0.5) * (points - 1.0),
            -4.0 * points * (points - 1.0),
            2.0 * points * (points - 0.5),
        ],
        1,
    )
    along_z = np.zeros((4, 16))
    for c in range(2):
        for p in range(8):
            for k in range(3):
                along_z[(2 * c + k) % 4, 8 * c + p] += basis[p, k]
    plane = np.einsum("nj,zc->jznc", basis, along_z).reshape(12, 128)
    matrix = np.zeros((128, 256), np.float32)
    matrix[16:28, :128] = plane
    matrix[80:92, 128:] = plane
    return matrix


def take_lanes(values, index):
    return jnp.take_along_axis(values, index, axis=1, mode="promise_in_bounds")


def stiffness_action(kappa, shifts):
    odd_x, odd_y, odd_z = shifts.odd

    def spread(values, axis):
        before = shifts.moved(values, axis, -1)
        return jnp.where(
            shifts.odd[axis], (2.0 / 3.0) * values, (1.0 / 6.0) * (values + before)
        )

    def spread_x(values):
        return jnp.where(
            odd_x,
            (2.0 / 3.0) * values,
            (1.0 / 6.0) * (values + shifts.slab(values, -1)),
        )

    over_x = spread_x(kappa)
    fields = (
        spread(spread(kappa, 1), 2) * (1.0 / 3.0),
        spread(over_x, 2) * (1.0 / 3.0),
        spread(over_x, 1) * (1.0 / 3.0),
    )
    centre = None
    pairs = []
    for axis in range(3):
        here = fields[axis]
        if axis == 0:
            before = shifts.slab(here, -1)
        else:
            before = shifts.moved(here, axis, -1)
        part = jnp.where(shifts.odd[axis], 16.0 * here, 7.0 * (here + before))
        centre = part if centre is None else centre + part
        pairs.append((here, jnp.where(shifts.odd[axis], here, before)))

    def act(values):
        total = centre * values
        for axis in range(3):
            ahead, behind = pairs[axis]
            one, two, back, back_two = shifts.neighbours(values, axis)
            odd = shifts.odd[axis]
            total = total + ahead * (jnp.where(odd, 0.0, two) - 8.0 * one)
            total = total + behind * (jnp.where(odd, 0.0, back_two) - 8.0 * back)
        return total

    return act


class Shifts:
    lane_axis = 1

    def lane_roll(self, values, by):
        return pltpu.roll(values, by % 128, self.lane_axis)

    def z_moved(self, values, by):
        z = self.z
        if by == 1:
            return jnp.where(z == 3, self.lane_roll(values, 3), self.lane_roll(values, -1))
        if by == -1:
            return jnp.where(z == 0, self.lane_roll(values, -3), self.lane_roll(values, 1))
        return jnp.where(z >= 2, self.lane_roll(values, 2), self.lane_roll(values, -2))

    def moved(self, values, axis, by):
        if axis == 1:
            return self.y_moved(values, by)
        return self.z_moved(values, by)

    def neighbours(self, values, axis):
        if axis == 0:
            other = self.other(values)
            ahead = jnp.where(self.odd[0], self.slab(other, 1), other)
            behind = jnp.where(self.odd[0], other, self.slab(other, -1))
            return ahead, self.slab(values, 1), behind, self.slab(values, -1)
        if axis == 1:
            return tuple(self.y_moved(values, by) for by in (1, 2, -1, -2))
        two = self.z_moved(values, 2)
        return self.z_moved(values, 1), two, self.z_moved(values, -1), two


class BrickShifts(Shifts):
    def __init__(self, shape):
        lane = lax.broadcasted_iota(jnp.int32, shape, 1)
        self.rows = shape[0]
        self.z = lane & 3
        self.odd = (lane >= 64, (lane & 4) != 0, (lane & 1) != 0)

    def y_moved(self, values, by):
        return self.lane_roll(values, -4 * by)

    def slab(self, values, by):
        return pltpu.roll(values, (-by) % self.rows, 0)

    def other(self, values):
        return self.lane_roll(values, 64)


class SlabShifts(Shifts):
    lane_axis = 2

    def __init__(self, shape):
        self.lane = lax.broadcasted_iota(jnp.int32, shape, 2)
        self.plane = lax.broadcasted_iota(jnp.int32, shape, 1) & 1
        self.z = self.lane & 3
        self.odd = (self.plane != 0, (self.lane & 4) != 0, (self.lane & 1) != 0)

    def y_moved(self, values, by):
        rolled = self.lane_roll(values, -4 * by)
        if by > 0:
            return jnp.where(
                self.lane < 128 - 4 * by, rolled, pltpu.roll(rolled, 6, 1)
            )
        return jnp.where(self.lane >= -4 * by, rolled, pltpu.roll(rolled, 2, 1))

    def slab(self, values, by):
        if by == 1:
            return jnp.concatenate([values[1:], values[:1]], 0)
        return jnp.concatenate([values[-1:], values[:-1]], 0)

    def other(self, values):
        return jnp.where(self.plane == 0, pltpu.roll(values, 7, 1), pltpu.roll(values, 1, 1))


def inverse_mass(shifts):
    odd_x, odd_y, odd_z = shifts.odd
    return (
        jnp.where(odd_x, 1.5, 3.0) * jnp.where(odd_y, 1.5, 3.0) * jnp.where(odd_z, 1.5, 3.0)
    )


def heat_step(field, heat, kappa, shifts):
    act = stiffness_action(kappa, shifts)
    inverse = inverse_mass(shifts)
    rate_one = (heat - act(field)) * inverse
    middle = field + STEP * rate_one
    rate_two = (heat - act(middle)) * inverse
    return field + (0.5 * STEP) * (rate_one + rate_two)


def blocks(values):
    return jnp.concatenate([values[:, 128 * q : 128 * q + 128] for q in range(4)], 0)


def lookup(table_ref, labels):
    low = labels & 127
    bits = [(labels & (256 << level)) != 0 for level in range(5)]

    def choose(first, level):
        if level < 0:
            return take_lanes(table_ref[8 * first : 8 * first + 8, :], low)
        return jnp.where(
            bits[level], choose(first + (1 << level), level - 1), choose(first, level - 1)
        )

    found = choose(0, 4)
    return jnp.where((labels & 128) != 0, found >> 12, found & 4095)


def exchange(
    groups,
    slabs,
    field_any,
    kappa_any,
    heat_any,
    solid_any,
    label_any,
    table_any,
    slot_any,
    seed_any,
    matrix_any,
    new_field_ref,
    solid_ref,
    planes,
    gathered,
    nucleation,
    side_ahead,
    side_behind,
    field_ref,
    kappa_ref,
    heat_ref,
    label_ref,
    table_ref,
    slot_ref,
    seed_ref,
    matrix_ref,
    outbox,
    inbox,
    near_field,
    near_heat,
    near_kappa,
    words,
    ahead_x,
    behind_x,
    ahead_y,
    behind_y,
    from_ahead_x,
    from_behind_x,
    from_ahead_y,
    from_behind_y,
    tally,
    edge_low,
    edge_high,
    load_sems,
    box_sems,
    row_sems,
    forward_sem,
    ready_sem,
    near_sems,
    near_send_sems,
    edge_recv_sems,
    edge_send_sems,
):
    def wait_messages(many, sem):
        size = tally.at[pl.ds(0, many)]
        pltpu.make_async_copy(size, size, sem).wait()

    loads = []
    for source, target, number in (
        (field_any, field_ref, 0),
        (heat_any, heat_ref, 0),
        (kappa_any, kappa_ref, 1),
        (table_any, table_ref, 2),
        (label_any, label_ref, 3),
        (solid_any, solid_ref, 4),
        (slot_any, slot_ref, 5),
        (seed_any, seed_ref, 5),
        (matrix_any, matrix_ref, 6),
    ):
        copy = pltpu.make_async_copy(source, target, load_sems.at[number])
        copy.start()
        loads.append(copy)
    g = lax.axis_index("grp")
    h = lax.axis_index("slab")
    g_next = lax.rem(g + 1, groups)
    g_prev = lax.rem(g + groups - 1, groups)

    ordered = g == groups - 1

    rows_y = slabs // 8
    early = 22

    def place(rank):
        at = jnp.where(rank < 2, rank + early, jnp.where(rank < early + 2, rank - 2, rank))
        fold = at >> 3
        row = jnp.where((fold & 1) == 1, (fold + 1) >> 1, 0 - (fold >> 1)) & (rows_y - 1)
        return 8 * row + (at & 7)

    def rank_of(other):
        row = other >> 3
        fold = jnp.where(
            row == 0, 0, jnp.where(row <= rows_y // 2, 2 * row - 1, 2 * (rows_y - row))
        )
        at = 8 * fold + (other & 7)
        return jnp.where(
            other >= slabs - 2, other - (slabs - 2), jnp.where(at < early, at + 2, at)
        )

    rank = rank_of(h)
    prev_upper = g == 0
    at_low, at_high = h <= 2, h >= slabs - 2
    sends_low = at_low & (g > 0) & jnp.logical_not(ordered)
    sends_high = at_high

    barrier = pltpu.get_barrier_semaphore()

    def greet(to_g, to_h):
        pl.semaphore_signal(barrier, inc=1, device_id=(to_g, to_h), device_id_type=MESH)

    greet(g_prev, h)
    for last in range(2):
        greet(g_prev, jnp.int32(slabs - 1 - last))

    @pl.when(jnp.logical_not(ordered))
    def _():
        greet(g_next, h)

    @pl.when(g < groups - 2)
    def _():
        for first in range(3):
            greet(g_next, jnp.int32(first))

    here = g * slabs + h
    count = groups * slabs
    near_to = {}
    for by in (1, -1, 2, -2):
        there = lax.rem(here + by + count, count)
        to_g, to_h = there // slabs, lax.rem(there, slabs)
        inside = to_g == g
        upper = jnp.where(
            inside, ordered & (rank_of(to_h) > rank), prev_upper if by < 0 else False
        )
        silent = ordered if by > 0 else False

        @pl.when(jnp.logical_not(inside | silent))
        def _(to_g=to_g, to_h=to_h):
            greet(to_g, to_h)

        near_to[by] = (to_g, to_h, inside, upper)

    def greet_rank(r, carry):
        greet(g, place(r))
        return carry

    lax.fori_loop(0, jnp.where(ordered, 0, rank), greet_rank, 0)
    lax.fori_loop(rank + 1, slabs, greet_rank, 0)

    wait_messages(8, load_sems.at[0])
    loads[2].wait()
    sub = lax.broadcasted_iota(jnp.int32, (8, 128), 0)
    lane = lax.broadcasted_iota(jnp.int32, (8, 128), 1)
    window = 8 * sub + (lane & 63)
    even_lane = lane < 64
    kappa_lane = (lane >= 44) & (lane < 56)
    kappa_rows = jnp.broadcast_to(kappa_ref[...], (8, 128))
    shifted_field = [pltpu.roll(field_ref[...], 16, 1), pltpu.roll(field_ref[...], 512 - 48, 1)]
    shifted_heat = [pltpu.roll(heat_ref[...], 16, 1), pltpu.roll(heat_ref[...], 512 - 48, 1)]

    def windows(shifted, m):
        part = shifted[m % 2][:, 128 * (m // 2) : 128 * (m // 2) + 128]
        even = take_lanes(jnp.broadcast_to(part[0:1], (8, 128)), window)
        odd = take_lanes(jnp.broadcast_to(part[1:2], (8, 128)), window)
        return jnp.where(even_lane, even, odd)

    for m in range(slabs // 8):
        outbox[8 * m : 8 * m + 8, 0:128] = windows(shifted_field, m)
        index = (2 * (8 * m + sub) - 4 + lane - 44) & 127
        outbox[8 * m : 8 * m + 8, 128:256] = jnp.where(
            kappa_lane, take_lanes(kappa_rows, index), windows(shifted_heat, m)
        )

    expected = (
        jnp.where(ordered, rank, slabs - 1)
        + jnp.where(g > 0, 2, 1)
        + jnp.where(sends_low, slabs, 0)
        + jnp.where(sends_high, slabs, 0)
    )
    for to_g, to_h, inside, upper in near_to.values():
        expected = expected + jnp.where(jnp.logical_not(inside | upper), 1, 0)

    first = ordered & sends_high

    @pl.when(first)
    def _():
        pl.semaphore_wait(barrier, expected)

    def remote(source, target, send_sem, recv_sem, device):
        return pltpu.make_async_remote_copy(
            src_ref=source,
            dst_ref=target,
            send_sem=send_sem,
            recv_sem=recv_sem,
            device_id=device,
            device_id_type=MESH,
        )

    def start_if(condition, copy):
        @pl.when(condition)
        def _():
            copy.start()

    def post(device, target_row, send_sem, recv_sem):
        return remote(
            outbox.at[pl.ds(device[1], 1), :],
            inbox.at[pl.ds(target_row, 1), :],
            send_sem,
            recv_sem,
            device,
        )

    near = {}
    for by in (1, -1, 2, -2):
        to_g, to_h, inside, upper = near_to[by]
        slot = {2: 0, 1: 1, -1: 2, -2: 3}[by]
        pairs = [(field_ref, near_field, slot, 0)]
        if by in (1, -1):
            pairs.append((heat_ref, near_heat, slot - 1, 1))
        if by != -2:
            pairs.append((kappa_ref, near_kappa, slot, 2))
        near[by] = [
            remote(
                source,
                target.at[place_],
                near_send_sems.at[kind // 2],
                near_sems.at[(0, 4, 6)[kind] + place_],
                (to_g, to_h),
            )
            for source, target, place_, kind in pairs
        ]
        for copy in near[by]:
            start_if(first & jnp.logical_not(upper), copy)

    slot_low = jnp.minimum(h, 2) + 2
    slot_high = jnp.maximum(h - (slabs - 2), 0)

    def fan_high():
        def body(to_h, carry):
            post((g_next, to_h), slot_high, box_sems.at[1], row_sems.at[0]).start()
            return carry

        lax.fori_loop(0, slabs, body, 0)

    pl.when(first)(fan_high)

    for copy in (*loads[3:6], loads[8]):
        copy.wait()
    wait_messages(2, load_sems.at[5])
    weight = 1 << (2 * lax.broadcasted_iota(jnp.int32, (6, 1), 0))
    codes = jnp.sum((table_ref[...] - 1) * weight, axis=0, keepdims=True)
    for row in range(31):
        low_half = codes[:, 256 * row : 256 * row + 128]
        high_half = codes[:, 256 * row + 128 : 256 * row + 256]
        words[8 * row : 8 * row + 8, :] = jnp.broadcast_to(
            low_half | (high_half << 12), (8, 128)
        )
    rest = jnp.concatenate([codes[:, 7936:8000], jnp.zeros((1, 64), jnp.int32)], 1)
    words[248:256, :] = jnp.broadcast_to(rest, (8, 128))

    edge_x = solid_ref.shape[0]

    def weighted_by(code, solid, d):
        return (0.25 * solid) * (((code >> (2 * d)) & 3) + 1).astype(jnp.float32)

    edge_low[...] = weighted_by(lookup(words, label_ref[0:8, :]), solid_ref[0:8, :], 0)
    edge_high[...] = weighted_by(
        lookup(words, label_ref[edge_x - 8 : edge_x, :]), solid_ref[edge_x - 8 : edge_x, :], 1
    )

    lane_c = lax.broadcasted_iota(jnp.int32, (CHUNK, 128), 1)
    depth = lane_c & 15

    def cells(c, carry):
        rows = pl.ds(pl.multiple_of(c * CHUNK, CHUNK), CHUNK)
        labels = label_ref[rows, :]
        code = jnp.concatenate(
            [lookup(words, labels[8 * k : 8 * k + 8]) for k in range(CHUNK // 8)], 0
        )
        quarter = 0.25 * solid_ref[rows, :]

        def weighted(d):
            return quarter * (((code >> (2 * d)) & 3) + 1).astype(jnp.float32)

        ahead_x[rows, :] = weighted(0)
        behind_x[rows, :] = weighted(1)
        up_y = weighted(2)
        down_y = weighted(3)
        up_z = weighted(4)
        down_z = weighted(5)
        gathered[rows, :] = (
            jnp.where(depth == 15, pltpu.roll(up_z, 15, 1), pltpu.roll(up_z, 127, 1))
            + jnp.where(depth == 0, pltpu.roll(down_z, 113, 1), pltpu.roll(down_z, 1, 1))
            + jnp.where(lane_c < 112, pltpu.roll(up_y, 112, 1), 0.0)
            + jnp.where(lane_c >= 16, pltpu.roll(down_y, 16, 1), 0.0)
        )
        mine = (lane_c >> 4) == c
        ahead_y[...] = jnp.where(mine, pltpu.roll(up_y, 16 * c, 1), ahead_y[...])
        behind_y[...] = jnp.where(
            mine, pltpu.roll(down_y, lax.rem(16 * c + 16, 128), 1), behind_y[...]
        )
        return carry

    ahead_y[...] = jnp.zeros(ahead_y.shape, jnp.float32)
    behind_y[...] = jnp.zeros(behind_y.shape, jnp.float32)
    chunks = edge_x // CHUNK
    x, y = (h >> 1) & 3, h >> 3
    hops = jnp.abs(x - 2) + jnp.abs(y - 4)
    last_ahead = jnp.maximum(chunks - 2 * x - jnp.where(y >= 4, 4, 0), 0)
    ahead = jnp.where(
        g == 0,
        chunks,
        jnp.where(
            first, 0, jnp.where(ordered, last_ahead, jnp.minimum(2 * hops, chunks))
        ),
    )
    lax.fori_loop(0, ahead, cells, 0)

    @pl.when(jnp.logical_not(first))
    def _():
        pl.semaphore_wait(barrier, expected)

    to_prev = remote(edge_low, from_ahead_x, edge_send_sems.at[1], edge_recv_sems.at[2], (g_prev, h))
    to_next = remote(edge_high, from_behind_x, edge_send_sems.at[1], edge_recv_sems.at[3], (g_next, h))
    start_if(jnp.logical_not(prev_upper), to_prev)
    to_next.start()

    for by in (1, -1, 2, -2):
        for copy in near[by]:
            start_if(jnp.logical_not(first | near_to[by][3]), copy)

    @pl.when(sends_low)
    def _():
        def body(to_h, carry):
            post((g_prev, to_h), slabs + slot_low, box_sems.at[1], row_sems.at[1]).start()
            return carry

        lax.fori_loop(0, slabs, body, 0)

    pl.when(jnp.logical_not(ordered) & sends_high)(fan_high)

    kind = jnp.where(at_low, 3, 2)
    own = pltpu.make_async_copy(
        outbox.at[pl.ds(h, 1), :], inbox.at[pl.ds(h + 2, 1), :], box_sems.at[kind]
    )
    own.start()

    def post_group(r, carry):
        post((g, place(r)), h + 2, box_sems.at[0], box_sems.at[kind]).start()
        return carry

    def answer(r, carry):
        pl.semaphore_signal(
            ready_sem, inc=1, device_id=(g, place(r)), device_id_type=MESH
        )
        return carry

    def post_above(step, carry):
        post((g, place(slabs - 1 - step)), h + 2, box_sems.at[0], box_sems.at[kind]).start()
        return carry

    lax.fori_loop(0, jnp.where(ordered, rank, 0), answer, 0)
    lax.fori_loop(0, jnp.where(ordered, 0, slabs - 1 - rank), post_above, 0)
    lax.fori_loop(0, rank, post_group, 0)

    lax.fori_loop(ahead, chunks, cells, 0)

    total = jnp.zeros((edge_x, 128), jnp.float32)
    cell_row = lax.broadcasted_iota(jnp.int32, (edge_x, 128), 0)
    cell_lane = lax.broadcasted_iota(jnp.int32, (128, 128), 0)
    for part in range(2):
        slots = slot_ref[part : part + 1, :]
        code = lookup(words, jnp.broadcast_to(seed_ref[part : part + 1, :], (8, 128)))
        level = jnp.full((8, 128), 6, jnp.int32)
        for d in range(6):
            level = level + ((code >> (2 * d)) & 3)
        level = level[0:1].astype(jnp.float32)
        at_row = jnp.where(cell_row == (slots >> 7), 1.0, 0.0).astype(jnp.bfloat16)
        at_lane = jnp.where(cell_lane == (slots & 127), level, 0.0).astype(jnp.bfloat16)
        total = total + lax.dot_general(
            at_row, at_lane, (((1,), (1,)), ((), ())), preferred_element_type=jnp.float32
        )
    nucleation[...] = total * (1.0 / 6.0)

    h_next = lax.rem(h + 1, slabs)
    h_prev = lax.rem(h + slabs - 1, slabs)
    down_y_copy = remote(
        ahead_y, from_ahead_y, edge_send_sems.at[0], edge_recv_sems.at[0], (g, h_prev)
    )
    up_y_copy = remote(
        behind_y, from_behind_y, edge_send_sems.at[0], edge_recv_sems.at[1], (g, h_next)
    )

    prev_above = ordered & (rank_of(h_prev) > rank)
    next_above = ordered & (rank_of(h_next) > rank)
    start_if(jnp.logical_not(prev_above), down_y_copy)
    start_if(jnp.logical_not(next_above), up_y_copy)

    gathered[0 : edge_x - 1, :] = gathered[0 : edge_x - 1, :] + ahead_x[1:edge_x, :]
    gathered[1:edge_x, :] = gathered[1:edge_x, :] + behind_x[0 : edge_x - 1, :]

    @pl.when(ordered & (rank < slabs - 1))
    def _():
        pl.semaphore_wait(ready_sem, slabs - 1 - rank)

    lax.fori_loop(0, jnp.where(ordered, slabs - 1 - rank, 0), post_above, 0)
    start_if(prev_above, down_y_copy)
    start_if(next_above, up_y_copy)
    for by in (1, -1, 2, -2):
        to_g, to_h, inside, upper = near_to[by]
        for copy in near[by]:
            start_if(upper & inside, copy)

    wait_messages(3, box_sems.at[3])

    to_prev_rows = [
        remote(
            inbox.at[pl.ds(2 + k, 1), :],
            inbox.at[pl.ds(slabs + 2 + k, 1), :],
            forward_sem,
            row_sems.at[1],
            (g_prev, h),
        )
        for k in range(3)
    ]
    for copy in to_prev_rows:
        start_if(ordered, copy)
    wait_messages(slabs - 3, box_sems.at[2])

    for by in (1, -1, 2, -2):
        to_g, to_h, inside, upper = near_to[by]

        @pl.when(upper & jnp.logical_not(inside))
        def _(by=by):
            for copy in near[-by]:
                copy.wait_recv()
            for copy in near[by]:
                copy.start()

    for by in (1, -1, 2, -2):

        @pl.when(near_to[-by][2] | jnp.logical_not(near_to[-by][3]))
        def _(by=by):
            for copy in near[by]:
                copy.wait_recv()

    zero = jnp.zeros((8, 128), jnp.float32)
    stacked_field = jnp.stack(
        [
            blocks(near_field[0]),
            blocks(near_field[1]),
            blocks(field_ref[...]),
            blocks(near_field[2]),
            blocks(near_field[3]),
        ],
        0,
    )
    stacked_heat = jnp.stack(
        [zero, blocks(near_heat[0]), blocks(heat_ref[...]), blocks(near_heat[1]), zero], 0
    )

    block_of = sub >> 1

    def expanded(row):
        index = block_of * 32 + (lane >> 3) * 2 + ((lane >> 1) & 1)
        return take_lanes(jnp.broadcast_to(row, (8, 128)), index)

    stacked_kappa = jnp.stack(
        [
            expanded(near_kappa[0]),
            expanded(near_kappa[1]),
            expanded(kappa_ref[...]),
            expanded(near_kappa[2]),
            zero,
        ],
        0,
    )
    moved = heat_step(
        stacked_field, stacked_heat, stacked_kappa, SlabShifts((5, 8, 128))
    )[2]
    for q in range(4):
        new_field_ref[:, 128 * q : 128 * q + 128] = moved[2 * q : 2 * q + 2, :]

    @pl.when(prev_upper)
    def _():
        to_next.wait_recv()
        to_prev.start()

    for copy in to_prev_rows:
        start_if(prev_upper, copy)

    wait_messages(2, row_sems.at[0])
    wait_messages(3, row_sems.at[1])
    shifts = BrickShifts((ROWS, 128))
    box_lane = lax.broadcasted_iota(jnp.int32, (ROWS, 128), 1)
    half = box_lane & 63
    brick_heat = inbox[:, 128:256]
    brick_kappa = take_lanes(
        brick_heat, jnp.minimum(44 + (half >> 3) * 2 + ((half >> 1) & 1), 55)
    )
    brick = heat_step(inbox[:, 0:128], brick_heat, brick_kappa, shifts)
    box_row = lax.broadcasted_iota(jnp.int32, (ROWS, 128), 0)
    wanted = (half >= 16) & (half < 28) & (box_row >= 2) & (box_row < slabs + 3)
    brick = pltpu.roll(jnp.where(wanted, brick, 0.0), ROWS - 2, 0)
    pair = jnp.dot(
        brick, matrix_ref[...], precision=HIGHEST, preferred_element_type=jnp.float32
    )
    planes[:, 0:256] = pair
    planes[:, 256:384] = pltpu.roll(pair[:, 0:128], ROWS - 1, 0)

    down_y_copy.wait_recv()
    up_y_copy.wait_recv()

    to_prev.wait_recv()

    @pl.when(jnp.logical_not(prev_upper))
    def _():
        to_next.wait_recv()

    gathered[edge_x - 1 : edge_x, :] = gathered[edge_x - 1 : edge_x, :] + from_ahead_x[0:1, :]
    gathered[0:1, :] = gathered[0:1, :] + from_behind_x[7:8, :]
    side_ahead[...] = from_ahead_y[...]
    side_behind[...] = from_behind_y[...]

    wait_messages(24, near_send_sems.at[0])
    pltpu.make_async_copy(near_kappa, near_kappa, near_send_sems.at[1]).wait()
    wait_messages(64, edge_send_sems.at[0])
    wait_messages(8, edge_send_sems.at[1])
    wait_messages(slabs - 1, box_sems.at[0])

    @pl.when(sends_low | sends_high)
    def _():
        wait_messages(slabs, box_sems.at[1])

    @pl.when(prev_upper | ordered)
    def _():
        wait_messages(3, forward_sem)


def finish(
    field_ref,
    solid_ref,
    planes,
    gathered,
    nucleation,
    side_ahead,
    side_behind,
    new_field_any,
    new_solid_any,
    result,
    sems,
):
    chunks = solid_ref.shape[0] // CHUNK
    field_out = pltpu.make_async_copy(field_ref, new_field_any, sems.at[1])
    field_out.start()
    sub = lax.broadcasted_iota(jnp.int32, (8, 128), 0)
    lane_c = lax.broadcasted_iota(jnp.int32, (CHUNK, 128), 1)
    point = (sub.astype(jnp.float32) + 0.5) * 0.125
    basis = (
        2.0 * (point - 0.5) * (point - 1.0),
        -4.0 * point * (point - 1.0),
        2.0 * point * (point - 0.5),
    )
    for c in range(chunks):
        rows = slice(c * CHUNK, (c + 1) * CHUNK)
        layer = planes[c * (CHUNK // 8) : (c + 1) * (CHUNK // 8), :]
        parts = []
        for k in range(CHUNK // 8):
            parts.append(
                basis[0] * layer[k : k + 1, 0:128]
                + basis[1] * layer[k : k + 1, 128:256]
                + basis[2] * layer[k : k + 1, 256:384]
            )
        under = jnp.maximum(-jnp.concatenate(parts, 0), 0.0)
        side = jnp.where(
            lane_c >= 112,
            pltpu.roll(side_ahead[...], (240 - 16 * c) % 128, 1),
            jnp.where(lane_c < 16, pltpu.roll(side_behind[...], (128 - 16 * c) % 128, 1), 0.0),
        )
        rate = under * (under * (gathered[rows, :] + side) + nucleation[rows, :])
        solid = solid_ref[rows, :]
        result[rows, :] = solid + (1.0 - solid) * (1.0 - jnp.exp(-rate))
        copy = pltpu.make_async_copy(result.at[rows, :], new_solid_any.at[rows, :], sems.at[0])
        copy.start()
    pltpu.make_async_copy(result, new_solid_any, sems.at[0]).wait()
    field_out.wait()


def solution(mesh):
    groups, slabs = mesh.shape["grp"], mesh.shape["slab"]
    matrix = interpolation_matrix()

    def body(field, kappa, heat, solid, label, table, slot, seed):
        vmem = pl.BlockSpec(memory_space=pltpu.VMEM)
        anywhere = pl.BlockSpec(memory_space=pl.ANY)
        edge_x = solid.shape[0]
        f32, i32 = jnp.float32, jnp.int32
        cells = (edge_x, 128)
        found = pl.pallas_call(
            functools.partial(exchange, groups, slabs),
            out_shape=(
                jax.ShapeDtypeStruct(field.shape, f32),
                jax.ShapeDtypeStruct(cells, f32),
                jax.ShapeDtypeStruct((ROWS, 384), f32),
                jax.ShapeDtypeStruct(cells, f32),
                jax.ShapeDtypeStruct(cells, f32),
                jax.ShapeDtypeStruct((CHUNK, 128), f32),
                jax.ShapeDtypeStruct((CHUNK, 128), f32),
            ),
            in_specs=[pl.BlockSpec(memory_space=pltpu.HBM)] * 9,
            out_specs=(vmem,) * 7,
            scratch_shapes=[
                pltpu.VMEM(field.shape, f32),
                pltpu.VMEM(kappa.shape, f32),
                pltpu.VMEM(heat.shape, f32),
                pltpu.VMEM(cells, i32),
                pltpu.VMEM(table.shape[::-1], i32),
                pltpu.VMEM((2, 128), i32),
                pltpu.VMEM((2, 128), i32),
                pltpu.VMEM(matrix.shape, f32),
                pltpu.VMEM((slabs, 256), f32),
                pltpu.VMEM((ROWS, 256), f32),
                pltpu.VMEM((4, 2, 512), f32),
                pltpu.VMEM((2, 2, 512), f32),
                pltpu.VMEM((3, 1, 128), f32),
                pltpu.VMEM((256, 128), i32),
                pltpu.VMEM(cells, f32),
                pltpu.VMEM(cells, f32),
                pltpu.VMEM((CHUNK, 128), f32),
                pltpu.VMEM((CHUNK, 128), f32),
                pltpu.VMEM((8, 128), f32),
                pltpu.VMEM((8, 128), f32),
                pltpu.VMEM((CHUNK, 128), f32),
                pltpu.VMEM((CHUNK, 128), f32),
                pltpu.VMEM((slabs, 2, 128), f32),
                pltpu.VMEM((8, 128), f32),
                pltpu.VMEM((8, 128), f32),
                pltpu.SemaphoreType.DMA((7,)),
                pltpu.SemaphoreType.DMA((4,)),
                pltpu.SemaphoreType.DMA((2,)),
                pltpu.SemaphoreType.DMA,
                pltpu.SemaphoreType.REGULAR,
                pltpu.SemaphoreType.DMA((9,)),
                pltpu.SemaphoreType.DMA((2,)),
                pltpu.SemaphoreType.DMA((4,)),
                pltpu.SemaphoreType.DMA((2,)),
            ],
            compiler_params=pltpu.CompilerParams(
                collective_id=0, has_side_effects=True, vmem_limit_bytes=16 << 20
            ),
        )(
            *(
                pltpu.with_memory_space_constraint(value, pltpu.HBM)
                for value in (
                    field,
                    kappa,
                    heat,
                    solid,
                    label,
                    table.T,
                    slot.reshape(2, 128),
                    seed.reshape(2, 128),
                    jnp.asarray(matrix),
                )
            )
        )
        return pl.pallas_call(
            finish,
            out_shape=(
                jax.ShapeDtypeStruct(field.shape, f32),
                jax.ShapeDtypeStruct(solid.shape, f32),
            ),
            in_specs=[vmem] * 7,
            out_specs=(anywhere, anywhere),
            scratch_shapes=[
                pltpu.VMEM(cells, f32),
                pltpu.SemaphoreType.DMA((2,)),
            ],
            compiler_params=pltpu.CompilerParams(vmem_limit_bytes=16 << 20),
        )(*found)

    in_specs = (
        P(("grp", "slab"), None),
        P(("grp", "slab"), None),
        P(("grp", "slab"), None),
        P("grp", "slab"),
        P("grp", "slab"),
        P(),
        P(("grp", "slab")),
        P(("grp", "slab")),
    )
    out_specs = (P(("grp", "slab"), None), P("grp", "slab"))
    return jax.shard_map(body, mesh=mesh, in_specs=in_specs, out_specs=out_specs, check_vma=False)
```

```python
import functools

import jax
import jax.numpy as jnp
import numpy as np
from jax import lax
from jax.experimental import pallas as pl
from jax.experimental.pallas import tpu as pltpu
from jax.sharding import PartitionSpec as P

MESH = pl.DeviceIdType.MESH
HIGHEST = lax.Precision.HIGHEST
STEP = 0.004
CHUNK = 64
ROWS = 72


def interpolation_matrix():
    points = (np.arange(8) + 0.5) / 8
    basis = np.stack(
        [
            2.0 * (points - 0.5) * (points - 1.0),
            -4.0 * points * (points - 1.0),
            2.0 * points * (points - 0.5),
        ],
        1,
    )
    along_z = np.zeros((4, 16))
    for c in range(2):
        for p in range(8):
            for k in range(3):
                along_z[(2 * c + k) % 4, 8 * c + p] += basis[p, k]
    plane = np.einsum("nj,zc->jznc", basis, along_z).reshape(12, 128)
    matrix = np.zeros((128, 256), np.float32)
    matrix[16:28, :128] = plane
    matrix[80:92, 128:] = plane
    return matrix


def take_lanes(values, index):
    return jnp.take_along_axis(values, index, axis=1, mode="promise_in_bounds")


def stiffness_action(kappa, shifts):
    odd_x, odd_y, odd_z = shifts.odd

    def spread(values, axis):
        before = shifts.moved(values, axis, -1)
        return jnp.where(
            shifts.odd[axis], (2.0 / 3.0) * values, (1.0 / 6.0) * (values + before)
        )

    def spread_x(values):
        return jnp.where(
            odd_x,
            (2.0 / 3.0) * values,
            (1.0 / 6.0) * (values + shifts.slab(values, -1)),
        )

    over_x = spread_x(kappa)
    fields = (
        spread(spread(kappa, 1), 2) * (1.0 / 3.0),
        spread(over_x, 2) * (1.0 / 3.0),
        spread(over_x, 1) * (1.0 / 3.0),
    )
    centre = None
    pairs = []
    for axis in range(3):
        here = fields[axis]
        if axis == 0:
            before = shifts.slab(here, -1)
        else:
            before = shifts.moved(here, axis, -1)
        part = jnp.where(shifts.odd[axis], 16.0 * here, 7.0 * (here + before))
        centre = part if centre is None else centre + part
        pairs.append((here, jnp.where(shifts.odd[axis], here, before)))

    def act(values):
        total = centre * values
        for axis in range(3):
            ahead, behind = pairs[axis]
            one, two, back, back_two = shifts.neighbours(values, axis)
            odd = shifts.odd[axis]
            total = total + ahead * (jnp.where(odd, 0.0, two) - 8.0 * one)
            total = total + behind * (jnp.where(odd, 0.0, back_two) - 8.0 * back)
        return total

    return act


class Shifts:
    lane_axis = 1

    def lane_roll(self, values, by):
        return pltpu.roll(values, by % 128, self.lane_axis)

    def z_moved(self, values, by):
        z = self.z
        if by == 1:
            return jnp.where(z == 3, self.lane_roll(values, 3), self.lane_roll(values, -1))
        if by == -1:
            return jnp.where(z == 0, self.lane_roll(values, -3), self.lane_roll(values, 1))
        return jnp.where(z >= 2, self.lane_roll(values, 2), self.lane_roll(values, -2))

    def moved(self, values, axis, by):
        if axis == 1:
            return self.y_moved(values, by)
        return self.z_moved(values, by)

    def neighbours(self, values, axis):
        if axis == 0:
            other = self.other(values)
            ahead = jnp.where(self.odd[0], self.slab(other, 1), other)
            behind = jnp.where(self.odd[0], other, self.slab(other, -1))
            return ahead, self.slab(values, 1), behind, self.slab(values, -1)
        if axis == 1:
            return tuple(self.y_moved(values, by) for by in (1, 2, -1, -2))
        two = self.z_moved(values, 2)
        return self.z_moved(values, 1), two, self.z_moved(values, -1), two


class BrickShifts(Shifts):
    def __init__(self, shape):
        lane = lax.broadcasted_iota(jnp.int32, shape, 1)
        self.rows = shape[0]
        self.z = lane & 3
        self.odd = (lane >= 64, (lane & 4) != 0, (lane & 1) != 0)

    def y_moved(self, values, by):
        return self.lane_roll(values, -4 * by)

    def slab(self, values, by):
        return pltpu.roll(values, (-by) % self.rows, 0)

    def other(self, values):
        return self.lane_roll(values, 64)


class SlabShifts(Shifts):
    lane_axis = 2

    def __init__(self, shape):
        self.lane = lax.broadcasted_iota(jnp.int32, shape, 2)
        self.plane = lax.broadcasted_iota(jnp.int32, shape, 1) & 1
        self.z = self.lane & 3
        self.odd = (self.plane != 0, (self.lane & 4) != 0, (self.lane & 1) != 0)

    def y_moved(self, values, by):
        rolled = self.lane_roll(values, -4 * by)
        if by > 0:
            return jnp.where(
                self.lane < 128 - 4 * by, rolled, pltpu.roll(rolled, 6, 1)
            )
        return jnp.where(self.lane >= -4 * by, rolled, pltpu.roll(rolled, 2, 1))

    def slab(self, values, by):
        if by == 1:
            return jnp.concatenate([values[1:], values[:1]], 0)
        return jnp.concatenate([values[-1:], values[:-1]], 0)

    def other(self, values):
        return jnp.where(self.plane == 0, pltpu.roll(values, 7, 1), pltpu.roll(values, 1, 1))


def inverse_mass(shifts):
    odd_x, odd_y, odd_z = shifts.odd
    return (
        jnp.where(odd_x, 1.5, 3.0) * jnp.where(odd_y, 1.5, 3.0) * jnp.where(odd_z, 1.5, 3.0)
    )


def heat_step(field, heat, kappa, shifts):
    act = stiffness_action(kappa, shifts)
    inverse = inverse_mass(shifts)
    rate_one = (heat - act(field)) * inverse
    middle = field + STEP * rate_one
    rate_two = (heat - act(middle)) * inverse
    return field + (0.5 * STEP) * (rate_one + rate_two)


def blocks(values):
    return jnp.concatenate([values[:, 128 * q : 128 * q + 128] for q in range(4)], 0)


def lookup(table_ref, labels):
    low = labels & 127
    bits = [(labels & (256 << level)) != 0 for level in range(5)]

    def choose(first, level):
        if level < 0:
            return take_lanes(table_ref[8 * first : 8 * first + 8, :], low)
        return jnp.where(
            bits[level], choose(first + (1 << level), level - 1), choose(first, level - 1)
        )

    found = choose(0, 4)
    return jnp.where((labels & 128) != 0, found >> 12, found & 4095)


def exchange(
    groups,
    slabs,
    field_any,
    kappa_any,
    heat_any,
    solid_any,
    label_any,
    table_any,
    slot_any,
    seed_any,
    matrix_any,
    new_field_ref,
    solid_ref,
    planes,
    gathered,
    nucleation,
    side_ahead,
    side_behind,
    field_ref,
    kappa_ref,
    heat_ref,
    label_ref,
    table_ref,
    slot_ref,
    seed_ref,
    matrix_ref,
    outbox,
    inbox,
    near_field,
    near_heat,
    near_kappa,
    words,
    ahead_x,
    behind_x,
    ahead_y,
    behind_y,
    from_ahead_x,
    from_behind_x,
    from_ahead_y,
    from_behind_y,
    tally,
    edge_low,
    edge_high,
    load_sems,
    box_sems,
    row_sems,
    forward_sem,
    ready_sem,
    near_sems,
    near_send_sems,
    edge_recv_sems,
    edge_send_sems,
):
    def wait_messages(many, sem):
        size = tally.at[pl.ds(0, many)]
        pltpu.make_async_copy(size, size, sem).wait()

    loads = []
    for source, target, number in (
        (field_any, field_ref, 0),
        (heat_any, heat_ref, 0),
        (kappa_any, kappa_ref, 1),
        (table_any, table_ref, 2),
        (label_any, label_ref, 3),
        (solid_any, solid_ref, 4),
        (slot_any, slot_ref, 5),
        (seed_any, seed_ref, 5),
        (matrix_any, matrix_ref, 6),
    ):
        copy = pltpu.make_async_copy(source, target, load_sems.at[number])
        copy.start()
        loads.append(copy)
    g = lax.axis_index("grp")
    h = lax.axis_index("slab")
    g_next = lax.rem(g + 1, groups)
    g_prev = lax.rem(g + groups - 1, groups)

    ordered = g == groups - 1

    rows_y = slabs // 8
    early = 22

    def place(rank):
        at = jnp.where(rank < 2, rank + early, jnp.where(rank < early + 2, rank - 2, rank))
        fold = at >> 3
        row = jnp.where((fold & 1) == 1, (fold + 1) >> 1, 0 - (fold >> 1)) & (rows_y - 1)
        return 8 * row + (at & 7)

    def rank_of(other):
        row = other >> 3
        fold = jnp.where(
            row == 0, 0, jnp.where(row <= rows_y // 2, 2 * row - 1, 2 * (rows_y - row))
        )
        at = 8 * fold + (other & 7)
        return jnp.where(
            other >= slabs - 2, other - (slabs - 2), jnp.where(at < early, at + 2, at)
        )

    rank = rank_of(h)
    prev_upper = g == 0
    at_low, at_high = h <= 2, h >= slabs - 2
    sends_low = at_low & (g > 0) & jnp.logical_not(ordered)
    sends_high = at_high

    barrier = pltpu.get_barrier_semaphore()

    def greet(to_g, to_h):
        pl.semaphore_signal(barrier, inc=1, device_id=(to_g, to_h), device_id_type=MESH)

    greet(g_prev, h)
    for last in range(2):
        greet(g_prev, jnp.int32(slabs - 1 - last))

    @pl.when(jnp.logical_not(ordered))
    def _():
        greet(g_next, h)

    @pl.when(g < groups - 2)
    def _():
        for first in range(3):
            greet(g_next, jnp.int32(first))

    here = g * slabs + h
    count = groups * slabs
    near_to = {}
    for by in (1, -1, 2, -2):
        there = lax.rem(here + by + count, count)
        to_g, to_h = there // slabs, lax.rem(there, slabs)
        inside = to_g == g
        upper = jnp.where(
            inside, ordered & (rank_of(to_h) > rank), prev_upper if by < 0 else False
        )
        silent = ordered if by > 0 else False

        @pl.when(jnp.logical_not(inside | silent))
        def _(to_g=to_g, to_h=to_h):
            greet(to_g, to_h)

        near_to[by] = (to_g, to_h, inside, upper)

    def greet_rank(r, carry):
        greet(g, place(r))
        return carry

    def greet_from(step, carry):
        greet(g, (h + step) & (slabs - 1))
        return carry

    def greet_slab(to_h, carry):
        greet(g, to_h)
        return carry

    first = ordered & sends_high
    lax.fori_loop(28, jnp.where(ordered, 28, slabs), greet_from, 0)
    lax.fori_loop(1, jnp.where(ordered, 1, 28), greet_from, 0)
    lax.fori_loop(0, jnp.where(first, slabs - 2, 0), greet_slab, 0)

    @pl.when(first & (rank == 0))
    def _():
        greet(g, jnp.int32(slabs - 1))

    lax.fori_loop(jnp.where(ordered & jnp.logical_not(first), rank + 1, slabs), slabs, greet_rank, 0)

    wait_messages(8, load_sems.at[0])
    loads[2].wait()
    sub = lax.broadcasted_iota(jnp.int32, (8, 128), 0)
    lane = lax.broadcasted_iota(jnp.int32, (8, 128), 1)
    window = 8 * sub + (lane & 63)
    even_lane = lane < 64
    kappa_lane = (lane >= 44) & (lane < 56)
    kappa_rows = jnp.broadcast_to(kappa_ref[...], (8, 128))
    shifted_field = [pltpu.roll(field_ref[...], 16, 1), pltpu.roll(field_ref[...], 512 - 48, 1)]
    shifted_heat = [pltpu.roll(heat_ref[...], 16, 1), pltpu.roll(heat_ref[...], 512 - 48, 1)]

    def windows(shifted, m):
        part = shifted[m % 2][:, 128 * (m // 2) : 128 * (m // 2) + 128]
        even = take_lanes(jnp.broadcast_to(part[0:1], (8, 128)), window)
        odd = take_lanes(jnp.broadcast_to(part[1:2], (8, 128)), window)
        return jnp.where(even_lane, even, odd)

    for m in range(slabs // 8):
        outbox[8 * m : 8 * m + 8, 0:128] = windows(shifted_field, m)
        index = (2 * (8 * m + sub) - 4 + lane - 44) & 127
        outbox[8 * m : 8 * m + 8, 128:256] = jnp.where(
            kappa_lane, take_lanes(kappa_rows, index), windows(shifted_heat, m)
        )

    expected = (
        jnp.where(ordered, rank, slabs - 1)
        + jnp.where(g > 0, 2, 1)
        + jnp.where(sends_low, slabs, 0)
        + jnp.where(sends_high, slabs, 0)
    )
    for to_g, to_h, inside, upper in near_to.values():
        expected = expected + jnp.where(jnp.logical_not(inside | upper), 1, 0)

    @pl.when(first)
    def _():
        pl.semaphore_wait(barrier, expected)

    def remote(source, target, send_sem, recv_sem, device):
        return pltpu.make_async_remote_copy(
            src_ref=source,
            dst_ref=target,
            send_sem=send_sem,
            recv_sem=recv_sem,
            device_id=device,
            device_id_type=MESH,
        )

    def start_if(condition, copy):
        @pl.when(condition)
        def _():
            copy.start()

    def post(device, target_row, send_sem, recv_sem):
        return remote(
            outbox.at[pl.ds(device[1], 1), :],
            inbox.at[pl.ds(target_row, 1), :],
            send_sem,
            recv_sem,
            device,
        )

    near = {}
    for by in (1, -1, 2, -2):
        to_g, to_h, inside, upper = near_to[by]
        slot = {2: 0, 1: 1, -1: 2, -2: 3}[by]
        pairs = [(field_ref, near_field, slot, 0)]
        if by in (1, -1):
            pairs.append((heat_ref, near_heat, slot - 1, 1))
        if by != -2:
            pairs.append((kappa_ref, near_kappa, slot, 2))
        near[by] = [
            remote(
                source,
                target.at[place_],
                near_send_sems.at[kind // 2],
                near_sems.at[(0, 4, 6)[kind] + place_],
                (to_g, to_h),
            )
            for source, target, place_, kind in pairs
        ]
        for copy in near[by]:
            start_if(first & jnp.logical_not(upper), copy)

    slot_low = jnp.minimum(h, 2) + 2
    slot_high = jnp.maximum(h - (slabs - 2), 0)

    def fan_high():
        def body(to_h, carry):
            post((g_next, to_h), slot_high, box_sems.at[1], row_sems.at[0]).start()
            return carry

        lax.fori_loop(0, slabs, body, 0)

    pl.when(first)(fan_high)

    for copy in (*loads[3:6], loads[8]):
        copy.wait()
    wait_messages(2, load_sems.at[5])
    weight = 1 << (2 * lax.broadcasted_iota(jnp.int32, (6, 1), 0))
    codes = jnp.sum((table_ref[...] - 1) * weight, axis=0, keepdims=True)
    for row in range(31):
        low_half = codes[:, 256 * row : 256 * row + 128]
        high_half = codes[:, 256 * row + 128 : 256 * row + 256]
        words[8 * row : 8 * row + 8, :] = jnp.broadcast_to(
            low_half | (high_half << 12), (8, 128)
        )
    rest = jnp.concatenate([codes[:, 7936:8000], jnp.zeros((1, 64), jnp.int32)], 1)
    words[248:256, :] = jnp.broadcast_to(rest, (8, 128))

    edge_x = solid_ref.shape[0]

    def weighted_by(code, solid, d):
        return (0.25 * solid) * (((code >> (2 * d)) & 3) + 1).astype(jnp.float32)

    edge_low[...] = weighted_by(lookup(words, label_ref[0:8, :]), solid_ref[0:8, :], 0)
    edge_high[...] = weighted_by(
        lookup(words, label_ref[edge_x - 8 : edge_x, :]), solid_ref[edge_x - 8 : edge_x, :], 1
    )

    lane_c = lax.broadcasted_iota(jnp.int32, (CHUNK, 128), 1)
    depth = lane_c & 15

    def cells(c, carry):
        rows = pl.ds(pl.multiple_of(c * CHUNK, CHUNK), CHUNK)
        labels = label_ref[rows, :]
        code = jnp.concatenate(
            [lookup(words, labels[8 * k : 8 * k + 8]) for k in range(CHUNK // 8)], 0
        )
        quarter = 0.25 * solid_ref[rows, :]

        def weighted(d):
            return quarter * (((code >> (2 * d)) & 3) + 1).astype(jnp.float32)

        ahead_x[rows, :] = weighted(0)
        behind_x[rows, :] = weighted(1)
        up_y = weighted(2)
        down_y = weighted(3)
        up_z = weighted(4)
        down_z = weighted(5)
        gathered[rows, :] = (
            jnp.where(depth == 15, pltpu.roll(up_z, 15, 1), pltpu.roll(up_z, 127, 1))
            + jnp.where(depth == 0, pltpu.roll(down_z, 113, 1), pltpu.roll(down_z, 1, 1))
            + jnp.where(lane_c < 112, pltpu.roll(up_y, 112, 1), 0.0)
            + jnp.where(lane_c >= 16, pltpu.roll(down_y, 16, 1), 0.0)
        )
        mine = (lane_c >> 4) == c
        ahead_y[...] = jnp.where(mine, pltpu.roll(up_y, 16 * c, 1), ahead_y[...])
        behind_y[...] = jnp.where(
            mine, pltpu.roll(down_y, lax.rem(16 * c + 16, 128), 1), behind_y[...]
        )
        return carry

    ahead_y[...] = jnp.zeros(ahead_y.shape, jnp.float32)
    behind_y[...] = jnp.zeros(behind_y.shape, jnp.float32)
    chunks = edge_x // CHUNK
    x, y = (h >> 1) & 3, h >> 3
    hops = jnp.abs(x - 2) + jnp.abs(y - 4)
    last_ahead = jnp.maximum(chunks - 2 * x - jnp.where(y >= 4, 4, 0), 0)
    ahead = jnp.where(
        g == 0,
        chunks,
        jnp.where(
            first, 0, jnp.where(ordered, last_ahead, jnp.minimum(2 * hops, chunks))
        ),
    )
    lax.fori_loop(0, ahead, cells, 0)

    @pl.when(jnp.logical_not(first))
    def _():
        pl.semaphore_wait(barrier, expected)

    to_prev = remote(edge_low, from_ahead_x, edge_send_sems.at[1], edge_recv_sems.at[2], (g_prev, h))
    to_next = remote(edge_high, from_behind_x, edge_send_sems.at[1], edge_recv_sems.at[3], (g_next, h))
    start_if(jnp.logical_not(prev_upper), to_prev)
    to_next.start()

    for by in (1, -1, 2, -2):
        for copy in near[by]:
            start_if(jnp.logical_not(first | near_to[by][3]), copy)

    @pl.when(sends_low)
    def _():
        def body(to_h, carry):
            post((g_prev, to_h), slabs + slot_low, box_sems.at[1], row_sems.at[1]).start()
            return carry

        lax.fori_loop(0, slabs, body, 0)

    pl.when(jnp.logical_not(ordered) & sends_high)(fan_high)

    kind = jnp.where(at_low, 3, 2)
    own = pltpu.make_async_copy(
        outbox.at[pl.ds(h, 1), :], inbox.at[pl.ds(h + 2, 1), :], box_sems.at[kind]
    )
    own.start()

    def post_group(r, carry):
        post((g, place(r)), h + 2, box_sems.at[0], box_sems.at[kind]).start()
        return carry

    def answer(r, carry):
        pl.semaphore_signal(
            ready_sem, inc=1, device_id=(g, place(r)), device_id_type=MESH
        )
        return carry

    def post_above(step, carry):
        post((g, place(slabs - 1 - step)), h + 2, box_sems.at[0], box_sems.at[kind]).start()
        return carry

    lax.fori_loop(0, jnp.where(ordered, rank, 0), answer, 0)
    lax.fori_loop(0, jnp.where(ordered, 0, slabs - 1 - rank), post_above, 0)
    lax.fori_loop(0, rank, post_group, 0)

    lax.fori_loop(ahead, chunks, cells, 0)

    total = jnp.zeros((edge_x, 128), jnp.float32)
    cell_row = lax.broadcasted_iota(jnp.int32, (edge_x, 128), 0)
    cell_lane = lax.broadcasted_iota(jnp.int32, (128, 128), 0)
    for part in range(2):
        slots = slot_ref[part : part + 1, :]
        code = lookup(words, jnp.broadcast_to(seed_ref[part : part + 1, :], (8, 128)))
        level = jnp.full((8, 128), 6, jnp.int32)
        for d in range(6):
            level = level + ((code >> (2 * d)) & 3)
        level = level[0:1].astype(jnp.float32)
        at_row = jnp.where(cell_row == (slots >> 7), 1.0, 0.0).astype(jnp.bfloat16)
        at_lane = jnp.where(cell_lane == (slots & 127), level, 0.0).astype(jnp.bfloat16)
        total = total + lax.dot_general(
            at_row, at_lane, (((1,), (1,)), ((), ())), preferred_element_type=jnp.float32
        )
    nucleation[...] = total * (1.0 / 6.0)

    h_next = lax.rem(h + 1, slabs)
    h_prev = lax.rem(h + slabs - 1, slabs)
    down_y_copy = remote(
        ahead_y, from_ahead_y, edge_send_sems.at[0], edge_recv_sems.at[0], (g, h_prev)
    )
    up_y_copy = remote(
        behind_y, from_behind_y, edge_send_sems.at[0], edge_recv_sems.at[1], (g, h_next)
    )

    prev_above = ordered & (rank_of(h_prev) > rank)
    next_above = ordered & (rank_of(h_next) > rank)
    start_if(jnp.logical_not(prev_above), down_y_copy)
    start_if(jnp.logical_not(next_above), up_y_copy)

    gathered[0 : edge_x - 1, :] = gathered[0 : edge_x - 1, :] + ahead_x[1:edge_x, :]
    gathered[1:edge_x, :] = gathered[1:edge_x, :] + behind_x[0 : edge_x - 1, :]

    @pl.when(ordered & (rank < slabs - 1))
    def _():
        pl.semaphore_wait(ready_sem, slabs - 1 - rank)

    lax.fori_loop(0, jnp.where(ordered, slabs - 1 - rank, 0), post_above, 0)
    start_if(prev_above, down_y_copy)
    start_if(next_above, up_y_copy)
    for by in (1, -1, 2, -2):
        to_g, to_h, inside, upper = near_to[by]
        for copy in near[by]:
            start_if(upper & inside, copy)

    wait_messages(3, box_sems.at[3])

    to_prev_rows = [
        remote(
            inbox.at[pl.ds(2 + k, 1), :],
            inbox.at[pl.ds(slabs + 2 + k, 1), :],
            forward_sem,
            row_sems.at[1],
            (g_prev, h),
        )
        for k in range(3)
    ]
    for copy in to_prev_rows:
        start_if(ordered, copy)
    wait_messages(slabs - 3, box_sems.at[2])

    for by in (1, -1, 2, -2):
        to_g, to_h, inside, upper = near_to[by]

        @pl.when(upper & jnp.logical_not(inside))
        def _(by=by):
            for copy in near[-by]:
                copy.wait_recv()
            for copy in near[by]:
                copy.start()

    for by in (1, -1, 2, -2):

        @pl.when(near_to[-by][2] | jnp.logical_not(near_to[-by][3]))
        def _(by=by):
            for copy in near[by]:
                copy.wait_recv()

    zero = jnp.zeros((8, 128), jnp.float32)
    stacked_field = jnp.stack(
        [
            blocks(near_field[0]),
            blocks(near_field[1]),
            blocks(field_ref[...]),
            blocks(near_field[2]),
            blocks(near_field[3]),
        ],
        0,
    )
    stacked_heat = jnp.stack(
        [zero, blocks(near_heat[0]), blocks(heat_ref[...]), blocks(near_heat[1]), zero], 0
    )

    block_of = sub >> 1

    def expanded(row):
        index = block_of * 32 + (lane >> 3) * 2 + ((lane >> 1) & 1)
        return take_lanes(jnp.broadcast_to(row, (8, 128)), index)

    stacked_kappa = jnp.stack(
        [
            expanded(near_kappa[0]),
            expanded(near_kappa[1]),
            expanded(kappa_ref[...]),
            expanded(near_kappa[2]),
            zero,
        ],
        0,
    )
    moved = heat_step(
        stacked_field, stacked_heat, stacked_kappa, SlabShifts((5, 8, 128))
    )[2]
    for q in range(4):
        new_field_ref[:, 128 * q : 128 * q + 128] = moved[2 * q : 2 * q + 2, :]

    @pl.when(prev_upper)
    def _():
        to_next.wait_recv()
        to_prev.start()

    for copy in to_prev_rows:
        start_if(prev_upper, copy)

    wait_messages(2, row_sems.at[0])
    wait_messages(3, row_sems.at[1])
    shifts = BrickShifts((ROWS, 128))
    box_lane = lax.broadcasted_iota(jnp.int32, (ROWS, 128), 1)
    half = box_lane & 63
    brick_heat = inbox[:, 128:256]
    brick_kappa = take_lanes(
        brick_heat, jnp.minimum(44 + (half >> 3) * 2 + ((half >> 1) & 1), 55)
    )
    brick = heat_step(inbox[:, 0:128], brick_heat, brick_kappa, shifts)
    box_row = lax.broadcasted_iota(jnp.int32, (ROWS, 128), 0)
    wanted = (half >= 16) & (half < 28) & (box_row >= 2) & (box_row < slabs + 3)
    brick = pltpu.roll(jnp.where(wanted, brick, 0.0), ROWS - 2, 0)
    pair = jnp.dot(
        brick, matrix_ref[...], precision=HIGHEST, preferred_element_type=jnp.float32
    )
    planes[:, 0:256] = pair
    planes[:, 256:384] = pltpu.roll(pair[:, 0:128], ROWS - 1, 0)

    down_y_copy.wait_recv()
    up_y_copy.wait_recv()

    to_prev.wait_recv()

    @pl.when(jnp.logical_not(prev_upper))
    def _():
        to_next.wait_recv()

    gathered[edge_x - 1 : edge_x, :] = gathered[edge_x - 1 : edge_x, :] + from_ahead_x[0:1, :]
    gathered[0:1, :] = gathered[0:1, :] + from_behind_x[7:8, :]
    side_ahead[...] = from_ahead_y[...]
    side_behind[...] = from_behind_y[...]

    wait_messages(24, near_send_sems.at[0])
    pltpu.make_async_copy(near_kappa, near_kappa, near_send_sems.at[1]).wait()
    wait_messages(64, edge_send_sems.at[0])
    wait_messages(8, edge_send_sems.at[1])
    wait_messages(slabs - 1, box_sems.at[0])

    @pl.when(sends_low | sends_high)
    def _():
        wait_messages(slabs, box_sems.at[1])

    @pl.when(prev_upper | ordered)
    def _():
        wait_messages(3, forward_sem)


def finish(
    field_ref,
    solid_ref,
    planes,
    gathered,
    nucleation,
    side_ahead,
    side_behind,
    new_field_any,
    new_solid_any,
    result,
    sems,
):
    chunks = solid_ref.shape[0] // CHUNK
    field_out = pltpu.make_async_copy(field_ref, new_field_any, sems.at[1])
    field_out.start()
    sub = lax.broadcasted_iota(jnp.int32, (8, 128), 0)
    lane_c = lax.broadcasted_iota(jnp.int32, (CHUNK, 128), 1)
    point = (sub.astype(jnp.float32) + 0.5) * 0.125
    basis = (
        2.0 * (point - 0.5) * (point - 1.0),
        -4.0 * point * (point - 1.0),
        2.0 * point * (point - 0.5),
    )
    for c in range(chunks):
        rows = slice(c * CHUNK, (c + 1) * CHUNK)
        layer = planes[c * (CHUNK // 8) : (c + 1) * (CHUNK // 8), :]
        parts = []
        for k in range(CHUNK // 8):
            parts.append(
                basis[0] * layer[k : k + 1, 0:128]
                + basis[1] * layer[k : k + 1, 128:256]
                + basis[2] * layer[k : k + 1, 256:384]
            )
        under = jnp.maximum(-jnp.concatenate(parts, 0), 0.0)
        side = jnp.where(
            lane_c >= 112,
            pltpu.roll(side_ahead[...], (240 - 16 * c) % 128, 1),
            jnp.where(lane_c < 16, pltpu.roll(side_behind[...], (128 - 16 * c) % 128, 1), 0.0),
        )
        rate = under * (under * (gathered[rows, :] + side) + nucleation[rows, :])
        solid = solid_ref[rows, :]
        result[rows, :] = solid + (1.0 - solid) * (1.0 - jnp.exp(-rate))
        copy = pltpu.make_async_copy(result.at[rows, :], new_solid_any.at[rows, :], sems.at[0])
        copy.start()
    pltpu.make_async_copy(result, new_solid_any, sems.at[0]).wait()
    field_out.wait()


def solution(mesh):
    groups, slabs = mesh.shape["grp"], mesh.shape["slab"]
    matrix = interpolation_matrix()

    def body(field, kappa, heat, solid, label, table, slot, seed):
        vmem = pl.BlockSpec(memory_space=pltpu.VMEM)
        anywhere = pl.BlockSpec(memory_space=pl.ANY)
        edge_x = solid.shape[0]
        f32, i32 = jnp.float32, jnp.int32
        cells = (edge_x, 128)
        found = pl.pallas_call(
            functools.partial(exchange, groups, slabs),
            out_shape=(
                jax.ShapeDtypeStruct(field.shape, f32),
                jax.ShapeDtypeStruct(cells, f32),
                jax.ShapeDtypeStruct((ROWS, 384), f32),
                jax.ShapeDtypeStruct(cells, f32),
                jax.ShapeDtypeStruct(cells, f32),
                jax.ShapeDtypeStruct((CHUNK, 128), f32),
                jax.ShapeDtypeStruct((CHUNK, 128), f32),
            ),
            in_specs=[pl.BlockSpec(memory_space=pltpu.HBM)] * 9,
            out_specs=(vmem,) * 7,
            scratch_shapes=[
                pltpu.VMEM(field.shape, f32),
                pltpu.VMEM(kappa.shape, f32),
                pltpu.VMEM(heat.shape, f32),
                pltpu.VMEM(cells, i32),
                pltpu.VMEM(table.shape[::-1], i32),
                pltpu.VMEM((2, 128), i32),
                pltpu.VMEM((2, 128), i32),
                pltpu.VMEM(matrix.shape, f32),
                pltpu.VMEM((slabs, 256), f32),
                pltpu.VMEM((ROWS, 256), f32),
                pltpu.VMEM((4, 2, 512), f32),
                pltpu.VMEM((2, 2, 512), f32),
                pltpu.VMEM((3, 1, 128), f32),
                pltpu.VMEM((256, 128), i32),
                pltpu.VMEM(cells, f32),
                pltpu.VMEM(cells, f32),
                pltpu.VMEM((CHUNK, 128), f32),
                pltpu.VMEM((CHUNK, 128), f32),
                pltpu.VMEM((8, 128), f32),
                pltpu.VMEM((8, 128), f32),
                pltpu.VMEM((CHUNK, 128), f32),
                pltpu.VMEM((CHUNK, 128), f32),
                pltpu.VMEM((slabs, 2, 128), f32),
                pltpu.VMEM((8, 128), f32),
                pltpu.VMEM((8, 128), f32),
                pltpu.SemaphoreType.DMA((7,)),
                pltpu.SemaphoreType.DMA((4,)),
                pltpu.SemaphoreType.DMA((2,)),
                pltpu.SemaphoreType.DMA,
                pltpu.SemaphoreType.REGULAR,
                pltpu.SemaphoreType.DMA((9,)),
                pltpu.SemaphoreType.DMA((2,)),
                pltpu.SemaphoreType.DMA((4,)),
                pltpu.SemaphoreType.DMA((2,)),
            ],
            compiler_params=pltpu.CompilerParams(
                collective_id=0, has_side_effects=True, vmem_limit_bytes=16 << 20
            ),
        )(
            *(
                pltpu.with_memory_space_constraint(value, pltpu.HBM)
                for value in (
                    field,
                    kappa,
                    heat,
                    solid,
                    label,
                    table.T,
                    slot.reshape(2, 128),
                    seed.reshape(2, 128),
                    jnp.asarray(matrix),
                )
            )
        )
        return pl.pallas_call(
            finish,
            out_shape=(
                jax.ShapeDtypeStruct(field.shape, f32),
                jax.ShapeDtypeStruct(solid.shape, f32),
            ),
            in_specs=[vmem] * 7,
            out_specs=(anywhere, anywhere),
            scratch_shapes=[
                pltpu.VMEM(cells, f32),
                pltpu.SemaphoreType.DMA((2,)),
            ],
            compiler_params=pltpu.CompilerParams(vmem_limit_bytes=16 << 20),
        )(*found)

    in_specs = (
        P(("grp", "slab"), None),
        P(("grp", "slab"), None),
        P(("grp", "slab"), None),
        P("grp", "slab"),
        P("grp", "slab"),
        P(),
        P(("grp", "slab")),
        P(("grp", "slab")),
    )
    out_specs = (P(("grp", "slab"), None), P("grp", "slab"))
    return jax.shard_map(body, mesh=mesh, in_specs=in_specs, out_specs=out_specs, check_vma=False)
```
